32 devices in a mesh: groups: 2 (over x), blk: 4 (over y, core), width: 4 (over z).
Axes of the slice: x: 2, y: 2, z: 4, core: 2. Of those that a mesh axis runs over, the one named last changes fastest.
Arguments:
- activations: float32 [8192, 8192], P(('groups', 'blk'), 'width'), parts along dimension 0, may hold values from -6 to 6
- query_grads: float32 [16, 8192, 128], P(('groups', 'blk'), 'width'), parts along dimension 0, may hold values from -0.0625 to 0.0625
- outgrad_proj: float32 [8192, 128], P(('groups', 'blk', 'width')), parts along dimension 0, may hold values from -0.6 to 0.6
- doc_ids: int32 [8192], P(('groups', 'blk', 'width')), parts along dimension 0, may hold values from 0 to 15, never falling along the last dimension, each value on 1 to 512 neighbouring positions
Outputs:
- token_scores: float32 [8192, 8], P(('groups', 'blk', 'width')), parts along dimension 0
- doc_scores: float32 [32, 8], P('groups'), parts along dimension 0
The draws below stay inside these ranges and needn't reach their ends.
There are 2 independent parts, one for each index of `groups`. The reference program is written for one: setup_inputs(seed, part) draws one part's arguments, and reference() takes and returns one part's arrays. A program takes and returns all parts, laid end to end along the dimension named above; each array names one. Nothing has to cross between parts.
Inputs may be any that keep to these rules, and one draw needn't show every extreme that they name: `doc_ids`: never falls along the tokens; every document 0 to 15 holds 1 to 512 tokens, one exactly 512.
All inputs are finite; a program needn't handle non-finite values.
Results may differ from the reference program's by a relative error of at most 0.000078.
Values sent between devices are 32-bit elements; how exact they have to be, the bound alone decides.
No kernel may reach another device: no remote copies, remote signals or barrier semaphores. Data moves between devices by JAX's collectives and lax.ppermute only.
A program may use at most 128 MiB of HBM per device.

```python
import math
import jax
import jax.numpy as jnp
import numpy as np
from jax import lax

D = 8192
R = 128
DOC_MOST = 512
TOKENS = 4096
NQ = 8
NDOC = 16


def block_levels(own_key, shape, split, low, top_value):
    loudness = 1.0
    for axis_at, blocks in split:
        steps = jax.random.uniform(jax.random.fold_in(jax.random.fold_in(own_key, 6), axis_at), (blocks,), jnp.float32, low / len(split), top_value / len(split))
        loudness = loudness * jnp.repeat(jnp.exp(steps), shape[axis_at] // blocks).reshape((-1,) + (1,) * (len(shape) - 1 - axis_at))
    return loudness


def split_up(number_of, total, most, lean):
    loads = [(1 << 20) // math.isqrt(rank ** lean) + 1 for rank in range(2, number_of + 1)]
    surplus, given = total - most - (number_of - 1), [1] * (number_of - 1)
    while surplus > 0:
        free = [i for i in range(number_of - 1) if given[i] < most]
        whole, left = sum([loads[i] for i in free]), surplus
        for i in free:
            addition = min(most - given[i], max(1, left * loads[i] // whole), surplus)
            given[i] = given[i] + addition
            surplus = surplus - addition
    return np.array([most] + given)


def ragged_sizes(rng, amount, total, most, lean):
    if amount == 2:
        one = jax.random.randint(rng, (), max(1, total - most), min(most, total - 1) + 1)
        return jnp.stack([one, total - one])
    sizes = jnp.asarray(split_up(amount, total, most, lean), jnp.int32)
    couples = (amount - 1) // 2
    donor, taker = sizes[1:1 + 2 * couples:2], sizes[2:2 + 2 * couples:2]
    slack = jnp.minimum(donor - 1, most - taker)
    moved = jax.random.randint(jax.random.fold_in(rng, 1), (couples,), 0, 1 << 20) % (slack + 1)
    sizes = sizes.at[1:1 + 2 * couples:2].set(donor - moved).at[2:2 + 2 * couples:2].set(taker + moved)
    return sizes[jax.random.permutation(jax.random.fold_in(rng, 2), amount)]


def normal_values(stream_key, dims, scale, reach, pieces=(), kind=jnp.bfloat16):
    values = jax.random.normal(stream_key, dims, jnp.float32) * scale
    if len(pieces) > 0:
        values = block_levels(stream_key, dims, pieces, -0.22, 0.18) * values
    return jnp.clip(values, min=-reach, max=reach).astype(kind)


def setup_inputs(seed: int = 0, part: int = 0) -> dict:
    splits = jax.random.split(jax.random.key(seed), 5)
    own_keys = jax.random.split(jax.random.fold_in(splits[4], part), 5)
    return {
        "activations": normal_values(own_keys[0], (TOKENS, D), 1.0, 6.0, ((0, 4), (1, 4)), jnp.float32),
        "query_grads": normal_values(own_keys[1], (NQ, D, R), D ** -0.5, 0.0625, ((0, 4), (1, 4)), jnp.float32),
        "outgrad_proj": normal_values(own_keys[2], (TOKENS, R), 0.0884, 0.6, ((0, 16),), jnp.float32),
        "doc_ids": jnp.searchsorted(jnp.cumsum(ragged_sizes(own_keys[3], NDOC, TOKENS, DOC_MOST, 2)), jnp.arange(TOKENS), side="right").astype(jnp.int32),
    }


def reference(activations, query_grads, outgrad_proj, doc_ids):

    def one_query(grad_mat):
        projected = jnp.dot(activations, grad_mat, precision=lax.Precision.HIGHEST, preferred_element_type=jnp.float32)
        return lax.optimization_barrier(jnp.sum(projected * outgrad_proj, axis=1))
    per_query = lax.map(one_query, query_grads)
    token_scores = jnp.transpose(per_query)
    doc_range = jnp.arange(NDOC, dtype=jnp.int32)
    onehot = (doc_ids[:, None] == doc_range[None, :]).astype(jnp.float32)
    doc_sums = jnp.dot(jnp.transpose(onehot), token_scores, precision=lax.Precision.HIGHEST, preferred_element_type=jnp.float32)
    doc_counts = lax.optimization_barrier(jnp.sum(onehot, axis=0))
    doc_scores = doc_sums / jnp.sqrt(doc_counts)[:, None]
    return (token_scores, doc_scores)
```

```python
import functools

import jax
import jax.numpy as jnp
from jax import lax
from jax.experimental import pallas as pl
from jax.experimental.pallas import tpu as pltpu
from jax.sharding import PartitionSpec as P

DOC_BLK = 4
LANES = 128
F32, BF16 = jnp.float32, jnp.bfloat16
VMEM = pl.BlockSpec(memory_space=pltpu.VMEM)
SMEM = pl.BlockSpec(memory_space=pltpu.SMEM)
LIMIT = 40 << 20


def split(x):
    high = x.astype(BF16)
    return high, (x - high.astype(F32)).astype(BF16)


def project(a, g):
    ah, al = split(a)
    gh, gl = split(g)
    dot = functools.partial(jnp.dot, preferred_element_type=F32)
    return dot(ah, gh) + dot(al, gh) + dot(ah, gl)


def score_rows(p, o, s_ref):
    r = o.shape[1]
    for i in range(s_ref.shape[0]):
        s_ref[i, :] = jnp.sum(p[:, i * r : (i + 1) * r] * o, axis=1)


def near_kernel(a_ref, g_ref, c_ref, o_ref, s_ref, acc_ref):
    k = pl.program_id(0)
    gs = [ref[q] for ref in (g_ref, c_ref) for q in range(ref.shape[0])]
    p = project(a_ref[...], jnp.concatenate(gs, axis=1))

    @pl.when(k == 0)
    def _():
        acc_ref[...] = p

    @pl.when(k > 0)
    def _():
        acc_ref[...] += p

    @pl.when(k == pl.num_programs(0) - 1)
    def _():
        score_rows(acc_ref[...], o_ref[...], s_ref)


def near_scores(a, g, c, o):
    t, d = a.shape
    nq, _, r = g.shape
    kc = min(d, 512)
    return pl.pallas_call(
        near_kernel,
        grid=(d // kc,),
        in_specs=[
            pl.BlockSpec((t, kc), lambda k: (0, k)),
            pl.BlockSpec((nq, kc, r), lambda k: (0, k, 0)),
            pl.BlockSpec((nq, kc, r), lambda k: (0, k, 0)),
            pl.BlockSpec((t, r), lambda k: (0, 0)),
        ],
        out_specs=pl.BlockSpec((2 * nq, t), lambda k: (0, 0)),
        out_shape=jax.ShapeDtypeStruct((2 * nq, t), F32),
        scratch_shapes=[pltpu.VMEM((t, 2 * nq * r), F32)],
        compiler_params=pltpu.CompilerParams(vmem_limit_bytes=LIMIT),
        cost_estimate=pl.CostEstimate(
            flops=12 * t * d * nq * r, bytes_accessed=4 * (t * d + 2 * nq * d * r), transcendentals=0
        ),
    )(a, g, c, o)


def far_kernel(a_ref, y_ref, c_ref, o_ref, prev_ref, s_ref):
    p = project(a_ref[...], jnp.concatenate([y_ref[...], c_ref[...]], axis=1))
    score_rows(p, o_ref[...], s_ref)
    s_ref[...] += prev_ref[...]


def far_specs(t, r, kc, at):
    return [
        pl.BlockSpec((t, kc), lambda i: (0, at)),
        pl.BlockSpec((kc, r), lambda i: (0, 0)),
        pl.BlockSpec((kc, r), lambda i: (0, 0)),
        pl.BlockSpec((t, r), lambda i: (0, 0)),
        pl.BlockSpec((2, t), lambda i: (0, 0)),
    ]


def far_cost(t, r, kc):
    return pl.CostEstimate(
        flops=12 * t * kc * r, bytes_accessed=4 * (t * kc + 2 * kc * r), transcendentals=0
    )


def far_scores(a, y, c, o, prev, start):
    t = a.shape[0]
    kc, r = y.shape
    return pl.pallas_call(
        far_kernel,
        grid=(1,),
        in_specs=far_specs(t, r, kc, start // kc),
        out_specs=pl.BlockSpec((2, t), lambda i: (0, 0)),
        out_shape=jax.ShapeDtypeStruct((2, t), F32),
        compiler_params=pltpu.CompilerParams(vmem_limit_bytes=LIMIT),
        cost_estimate=far_cost(t, r, kc),
    )(a, y, c, o, prev)


def per_device(a, g, o, ids):
    nb, nw = lax.axis_size("blk"), lax.axis_size("width")
    b, w = lax.axis_index("blk"), lax.axis_index("width")
    nq, d, r = g.shape
    t = a.shape[0]
    own = o.shape[0]
    docs = DOC_BLK * nb
    pairs = lambda n, k: [(i, i ^ k) for i in range(n)]
    to_core = lambda x: lax.ppermute(x, "blk", pairs(nb, 1))

    sizes = [d // 4] * 4
    pieces = []
    for q in range(nq):
        at = 0
        for n in sizes:
            pieces.append((q, at, n))
            at += n
    arrived = {}
    for j in range(2, nb, 2):
        for q, at, n in pieces:
            arrived[j, q, at] = lax.ppermute(g[q, at : at + n], "blk", pairs(nb, j))
    core = to_core(g)

    rows = own // LANES
    flat = ids.astype(F32).reshape(rows, LANES)
    mine = jnp.concatenate([o, flat], axis=0)
    all_o = jnp.zeros((t, r), F32)
    all_ids = jnp.zeros((t // LANES, LANES), F32)
    for k in range(nw):
        got = lax.ppermute(mine, "width", pairs(nw, k)) if k else mine
        src = w ^ k
        all_o = lax.dynamic_update_slice(all_o, got[:own], (src * own, 0))
        all_ids = lax.dynamic_update_slice(all_ids, got[own:], (src * rows, 0))

    near = near_scores(a, g, core, all_o)
    scores = {0: near[:nq], 1: near[nq:]}
    for j in range(2, nb, 2):
        per_q = []
        for q in range(nq):
            s = jnp.zeros((2, t), F32)
            for q2, at, n in pieces:
                if q2 == q:
                    y = arrived[j, q, at]
                    s = far_scores(a, y, to_core(y), all_o, s, at)
            per_q.append(s)
        scores[j] = jnp.stack([s[0] for s in per_q])
        scores[j + 1] = jnp.stack([s[1] for s in per_q])

    blocks = [scores[k] for k in range(nb)]
    bit = 1
    while bit < nb:
        swap = (b & bit) != 0
        blocks = [jnp.where(swap, blocks[i ^ bit], blocks[i]) for i in range(nb)]
        bit *= 2
    s = jnp.concatenate(blocks, axis=0)

    token_ids = all_ids.reshape(t)
    ndoc = jnp.arange(docs, dtype=F32)
    onehot = (token_ids[:, None] == ndoc[None, :]).astype(F32)
    doc = jnp.dot(s, onehot, precision=lax.Precision.HIGHEST, preferred_element_type=F32)
    count = jnp.sum((ids[:, None] == jnp.arange(docs, dtype=jnp.int32)[None, :]).astype(F32), axis=0)
    doc = jnp.concatenate([doc, jnp.broadcast_to(count[None, :], doc.shape)], axis=1)

    k = 1
    while k < nb:
        doc = doc + lax.ppermute(doc, "blk", pairs(nb, k))
        k *= 2
    k = nw // 2
    while k:
        half = s.shape[1] // 2
        low = (w & k) == 0
        keep = jnp.where(low, s[:, :half], s[:, half:])
        send = jnp.where(low, s[:, half:], s[:, :half])
        got = lax.ppermute(jnp.concatenate([send, doc], axis=1), "width", pairs(nw, k))
        s = keep + got[:, :half]
        doc = doc + got[:, half:]
        k //= 2
    doc_scores = (doc[:, :docs] / jnp.sqrt(doc[:, docs:])).T
    return (s.T, doc_scores)


def solution(mesh):
    return jax.shard_map(
        per_device,
        mesh=mesh,
        in_specs=(
            P(("groups", "blk"), "width"),
            P(("groups", "blk"), "width", None),
            P(("groups", "blk", "width"), None),
            P(("groups", "blk", "width")),
        ),
        out_specs=(P(("groups", "blk", "width"), None), P("groups", None)),
        check_vma=False,
    )
```

```python
import functools

import jax
import jax.numpy as jnp
from jax import lax
from jax.experimental import pallas as pl
from jax.experimental.pallas import tpu as pltpu
from jax.sharding import PartitionSpec as P

DOC_BLK = 4
LANES = 128
F32, BF16 = jnp.float32, jnp.bfloat16
PARTS = (2, 4, 8, 16, 16)


def split(x):
    high = x.astype(BF16)
    return high, (x - high.astype(F32)).astype(BF16)


def project(a, gh, gl):
    ah, al = split(a)
    dot = functools.partial(jnp.dot, preferred_element_type=F32)
    return dot(ah, gh) + dot(al, gh) + dot(ah, gl)


def score_kernel(first, n_a, *refs):
    a_refs, refs = refs[:n_a], refs[n_a:]
    o_refs, refs = refs[:n_a], refs[n_a:]
    g_ref, prev_ref, s_ref, *acc = refs
    k = pl.program_id(0)
    last = pl.num_programs(0) - 1
    nq = g_ref.shape[0]
    gh, gl = split(jnp.concatenate([g_ref[q] for q in range(nq)], axis=1))

    @pl.when(k == last)
    def _():
        s_ref[...] = prev_ref[...]

    for h, (a_ref, o_ref) in enumerate(zip(a_refs, o_refs)):
        t, r = o_ref.shape
        p = project(a_ref[...], gh, gl)

        def finish(p, h=h, o_ref=o_ref):
            o = o_ref[...]
            for q in range(nq):
                row = jnp.sum(p[:, q * r : (q + 1) * r] * o, axis=1)
                s_ref[first + q, h * t : (h + 1) * t] += row

        if not acc:
            finish(p)
            continue
        acc_ref = acc[0].at[h]

        @pl.when(k == 0)
        def _(acc_ref=acc_ref, p=p):
            acc_ref[...] = p

        @pl.when((k > 0) & (k < last))
        def _(acc_ref=acc_ref, p=p):
            acc_ref[...] += p

        @pl.when(k == last)
        def _(acc_ref=acc_ref, p=p, finish=finish):
            finish(acc_ref[...] + p)


def add_scores(s, activations, outgrads, g, start, first):
    t = activations[0].shape[0]
    nq, n, r = g.shape
    kc = min(n, 512)
    steps, at = n // kc, start // kc
    n_a = len(activations)
    whole = pl.BlockSpec((s.shape[0], n_a * t), lambda i: (0, 0))
    return pl.pallas_call(
        functools.partial(score_kernel, first, n_a),
        grid=(steps,),
        in_specs=[pl.BlockSpec((t, kc), lambda i: (0, at + i))] * n_a
        + [pl.BlockSpec((t, r), lambda i: (0, 0))] * n_a
        + [pl.BlockSpec((nq, kc, r), lambda i: (0, i, 0)), whole],
        out_specs=whole,
        out_shape=jax.ShapeDtypeStruct(s.shape, F32),
        scratch_shapes=[pltpu.VMEM((n_a, t, nq * r), F32)] if steps > 1 else [],
        compiler_params=pltpu.CompilerParams(vmem_limit_bytes=40 << 20),
        cost_estimate=pl.CostEstimate(flops=1, bytes_accessed=1, transcendentals=0),
    )(*activations, *outgrads, g, s)


def per_device(a, g, o, ids):
    nb, nw = lax.axis_size("blk"), lax.axis_size("width")
    b, w = lax.axis_index("blk"), lax.axis_index("width")
    nq, d, r = g.shape
    t = a.shape[0]
    own = o.shape[0]
    docs = DOC_BLK * nb
    pairs = lambda n, k: [(i, i ^ k) for i in range(n)]
    to_core = lambda x: lax.ppermute(x, "blk", pairs(nb, 1))

    def after(x, *others):
        return lax.optimization_barrier((x, *others))[0]

    pieces = []
    for j in range(2, nb, 2):
        at = 0
        for part in PARTS:
            n = max(d // part, LANES)
            if at < d:
                pieces.append((j, at, n))
            at += n

    def cut(i, source):
        _, at, n = pieces[i]
        return source[:, at : at + n]

    def send(i, x):
        return lax.ppermute(x, "blk", pairs(nb, pieces[i][0]))

    first = cut(0, g)
    arrived = [send(0, first)]
    g1, a1 = lax.optimization_barrier((g, a, first))[:2]
    arrived.append(send(1, cut(1, g1)))
    a_other = to_core(a1)

    rows = own // LANES
    flat = ids.astype(F32).reshape(rows, LANES)
    flat_other = to_core(after(flat, first))
    mine = after(jnp.concatenate([o, flat], axis=0), flat_other)
    table = jnp.zeros((t + t // LANES, LANES), F32)
    for k in range(nw):
        got = lax.ppermute(mine, "width", pairs(nw, k)) if k else mine
        src = w ^ k
        table = lax.dynamic_update_slice(table, got[:own], (src * own, 0))
        table = lax.dynamic_update_slice(table, got[own:], (t + src * rows, 0))
    other = to_core(table)

    zero = jnp.zeros((nb // 2 * nq, t), F32)
    mine_s = add_scores(zero, [a], [table], g, 0, 0)
    other_s = add_scores(zero, [a_other], [other], after(g, mine_s), 0, 0)
    s = jnp.concatenate([mine_s, other_s], axis=1)
    for i, (j, at, n) in enumerate(pieces):
        if i + 2 < len(pieces):
            arrived.append(send(i + 2, cut(i + 2, after(g, s))))
        s = add_scores(s, [a, a_other], [table, other], arrived[i], at, j // 2 * nq)

    number = jnp.arange(docs, dtype=F32)
    marks = lambda x: (x.reshape(-1)[:, None] == number[None, :]).astype(F32)
    count = jnp.sum(marks(flat), axis=0) + jnp.sum(marks(flat_other), axis=0)
    onehot = marks(jnp.concatenate([table[t:], other[t:]], axis=0))
    doc = jnp.dot(s, onehot, precision=lax.Precision.HIGHEST, preferred_element_type=F32)

    keep = jnp.concatenate([s[:, :t], doc], axis=1)
    got = to_core(jnp.concatenate([s[:, t:], doc], axis=1))
    blocks = []
    for k in range(0, nb // 2 * nq, nq):
        blocks += [keep[k : k + nq], got[k : k + nq]]
    bit = 1
    while bit < nb:
        swap = (b & bit) != 0
        blocks = [jnp.where(swap, blocks[i ^ bit], blocks[i]) for i in range(nb)]
        bit *= 2
    s = jnp.concatenate(blocks, axis=0)
    s, doc = s[:, :t], s[:, t:]
    doc = jnp.concatenate([doc, jnp.broadcast_to(count[None, :], doc.shape)], axis=1)

    k = 2
    while k < nb:
        doc = doc + lax.ppermute(doc, "blk", pairs(nb, k))
        k *= 2
    k = nw // 2
    while k:
        half = s.shape[1] // 2
        low = (w & k) == 0
        keep = jnp.where(low, s[:, :half], s[:, half:])
        give = jnp.where(low, s[:, half:], s[:, :half])
        got = lax.ppermute(jnp.concatenate([give, doc], axis=1), "width", pairs(nw, k))
        s = keep + got[:, :half]
        doc = doc + got[:, half:]
        k //= 2
    doc_scores = (doc[:, :docs] / jnp.sqrt(doc[:, docs:])).T
    return (s.T, doc_scores)


def solution(mesh):
    return jax.shard_map(
        per_device,
        mesh=mesh,
        in_specs=(
            P(("groups", "blk"), "width"),
            P(("groups", "blk"), "width", None),
            P(("groups", "blk", "width"), None),
            P(("groups", "blk", "width")),
        ),
        out_specs=(P(("groups", "blk", "width"), None), P("groups", None)),
        check_vma=False,
    )
```

```python
import functools

import jax
import jax.numpy as jnp
from jax import lax
from jax.experimental import pallas as pl
from jax.experimental.pallas import tpu as pltpu
from jax.sharding import PartitionSpec as P

DOC_BLK = 4
LANES = 128
F32, BF16 = jnp.float32, jnp.bfloat16
TILE = 256
PARTS = (2, 4, 8, 16, 16)
VMEM = pl.BlockSpec(memory_space=pltpu.VMEM)
HBM = pl.BlockSpec(memory_space=pltpu.HBM)
PARAMS = pltpu.CompilerParams(vmem_limit_bytes=16 << 20)
COST = pl.CostEstimate(flops=1, bytes_accessed=1, transcendentals=0)


def split(x):
    high = x.astype(BF16)
    return high, (x - high.astype(F32)).astype(BF16)


def in_hbm(x):
    return pltpu.with_memory_space_constraint(x, pltpu.HBM)


def cut_kernel(pieces, g_ref, *refs):
    outs, sems = refs[:-1], refs[-1]
    copies = [
        pltpu.make_async_copy(g_ref.at[:, at : at + n], out, sems.at[i])
        for i, ((at, n), out) in enumerate(zip(pieces, outs))
    ]
    for copy in copies:
        copy.start()
    for copy in copies:
        copy.wait()


def cut(g, pieces):
    nq, _, r = g.shape
    return pl.pallas_call(
        functools.partial(cut_kernel, pieces),
        in_specs=[HBM],
        out_specs=[VMEM] * len(pieces),
        out_shape=[jax.ShapeDtypeStruct((nq, n, r), F32) for _, n in pieces],
        scratch_shapes=[pltpu.SemaphoreType.DMA((len(pieces),))],
        compiler_params=PARAMS,
        cost_estimate=COST,
    )(in_hbm(g))


def weigh(g_ref, step):
    nq, n, _ = g_ref.shape
    return [
        split(jnp.concatenate([g_ref[q, k : k + step] for q in range(nq)], axis=1))
        for k in range(0, n, step)
    ]


def score_tile(a, weights, o, step):
    dot = functools.partial(jnp.dot, preferred_element_type=F32)
    p = None
    for i, (gh, gl) in enumerate(weights):
        gh, gl = gh[...], gl[...]
        ah, al = split(a[:, i * step : (i + 1) * step])
        if step < 256:
            part = dot(jnp.concatenate([ah, al, ah], axis=1), jnp.concatenate([gh, gh, gl], axis=0))
        else:
            part = dot(ah, gh) + dot(al, gh) + dot(ah, gl)
        p = part if p is None else p + part
    r = o.shape[1]
    return [jnp.sum(p[:, q : q + r] * o, axis=1) for q in range(0, p.shape[1], r)]


def stream_kernel(first, staged, *refs):
    a_refs, o_refs, refs = refs[:2], refs[2:4], refs[4:]
    g_ref, prev_ref, s_ref, *stage_refs, high_ref, low_ref = refs
    tile, n = a_refs[0].shape
    t = s_ref.shape[1] // 2
    i = pl.program_id(0)
    step = high_ref.shape[1]

    @pl.when(i == 0)
    def _():
        s_ref[...] = prev_ref[...]
        for k, (gh, gl) in enumerate(weigh(g_ref, step)):
            high_ref[k] = gh
            low_ref[k] = gl

    weights = [(high_ref.at[k], low_ref.at[k]) for k in range(n // step)]
    for h in range(2):
        a = a_refs[h][...]
        at = pl.multiple_of(h * t + i * tile, tile)
        for q, row in enumerate(score_tile(a, weights, o_refs[h][...], step)):
            s_ref[first + q, pl.ds(at, tile)] += row
        if staged:
            stage_refs[h][...] = a[:, n - staged :]


def stream_scores(s, activations, outgrads, g, start, first, staged=0):
    t = activations[0].shape[0]
    nq, n, r = g.shape
    tile = min(t, TILE)
    step = min(n, 512)
    col = start // n
    whole = pl.BlockSpec(s.shape, lambda i: (0, 0))
    stage = jax.ShapeDtypeStruct((t, staged), F32)
    out = pl.pallas_call(
        functools.partial(stream_kernel, first, staged),
        grid=(t // tile,),
        in_specs=[pl.BlockSpec((tile, n), lambda i: (i, col))] * 2
        + [pl.BlockSpec((tile, r), lambda i: (i, 0))] * 2
        + [pl.BlockSpec((nq, n, r), lambda i: (0, 0, 0), pipeline_mode=pl.Buffered(1)), whole],
        out_specs=[whole] + [pl.BlockSpec((tile, staged), lambda i: (i, 0))] * (2 if staged else 0),
        out_shape=[jax.ShapeDtypeStruct(s.shape, F32)] + [stage] * (2 if staged else 0),
        scratch_shapes=[pltpu.VMEM((n // step, step, nq * r), BF16)] * 2,
        compiler_params=PARAMS,
        cost_estimate=COST,
    )(*[in_hbm(a) for a in activations], *outgrads, g, s)
    return out if staged else out[0]


def staged_kernel(start, first, *refs):
    a_refs, o_refs, (g_ref, prev_ref, s_ref) = refs[:2], refs[2:4], refs[4:]
    n = g_ref.shape[1]
    t = a_refs[0].shape[0]
    tile = min(t, 256)
    weights = weigh(g_ref, n)
    s_ref[...] = prev_ref[...]
    for h in range(2):
        for m in range(0, t, tile):
            a = a_refs[h][m : m + tile, start : start + n]
            at = h * t + m
            for q, row in enumerate(score_tile(a, weights, o_refs[h][m : m + tile, :], n)):
                s_ref[first + q, at : at + tile] += row


def staged_scores(s, stages, outgrads, g, start, first):
    return pl.pallas_call(
        functools.partial(staged_kernel, start, first),
        in_specs=[VMEM] * 6,
        out_specs=VMEM,
        out_shape=jax.ShapeDtypeStruct(s.shape, F32),
        compiler_params=PARAMS,
        cost_estimate=COST,
    )(*stages, *outgrads, g, s)


def per_device(a, g, o, ids):
    nb, nw = lax.axis_size("blk"), lax.axis_size("width")
    b, w = lax.axis_index("blk"), lax.axis_index("width")
    nq, d, r = g.shape
    t = a.shape[0]
    own = o.shape[0]
    docs = DOC_BLK * nb
    pairs = lambda n, k: [(i, i ^ k) for i in range(n)]
    to_core = lambda x: lax.ppermute(x, "blk", pairs(nb, 1))

    def after(x, *others):
        return lax.optimization_barrier((x, *others))[0]

    pieces, at = [], 0
    for part in PARTS:
        n = max(d // part, LANES)
        if at < d:
            pieces.append((at, n))
        at += n
    cuts = cut(g, pieces[:1])
    ids_other = to_core(after(ids, cuts[0]))
    cuts += cut(after(g, ids_other), pieces[1:])
    sends = [(j, at, x) for j in range(2, nb, 2) for (at, _), x in zip(pieces, cuts)]

    def send(i, *others):
        j, _, x = sends[i]
        return lax.ppermute(after(x, *others), "blk", pairs(nb, j))

    arrived = [send(0), send(1)]
    a_other = to_core(after(a, ids_other))

    rows = own // LANES
    flat = ids.astype(F32).reshape(rows, LANES)
    mine = after(jnp.concatenate([o, flat], axis=0), ids_other)
    table = jnp.zeros((t + t // LANES, LANES), F32)
    for k in range(nw):
        got = lax.ppermute(mine, "width", pairs(nw, k)) if k else mine
        src = w ^ k
        table = lax.dynamic_update_slice(table, got[:own], (src * own, 0))
        table = lax.dynamic_update_slice(table, got[own:], (t + src * rows, 0))
    other = to_core(table)

    both, outgrads = [a, a_other], [table, other]
    s = jnp.zeros((nb // 2 * nq, 2 * t), F32)
    late = d - pieces[-3][0]
    s, *stages = stream_scores(s, both, outgrads, g, 0, 0, late)
    for i, (j, at, x) in enumerate(sends):
        if i + 2 < len(sends):
            arrived.append(send(i + 2, s))
        first = j // 2 * nq
        if at < d - late:
            s = stream_scores(s, both, outgrads, arrived[i], at, first)
        else:
            s = staged_scores(s, stages, outgrads, arrived[i], at - (d - late), first)

    number = jnp.arange(docs, dtype=F32)
    marks = lambda x: (x.reshape(-1)[:, None] == number[None, :]).astype(F32)
    count = jnp.sum(marks(flat), axis=0) + jnp.sum(marks(ids_other.astype(F32)), axis=0)
    onehot = marks(jnp.concatenate([table[t:], other[t:]], axis=0))
    doc = jnp.dot(s, onehot, precision=lax.Precision.HIGHEST, preferred_element_type=F32)

    keep = jnp.concatenate([s[:, :t], doc], axis=1)
    got = to_core(jnp.concatenate([s[:, t:], doc], axis=1))
    blocks = []
    for k in range(0, nb // 2 * nq, nq):
        blocks += [keep[k : k + nq], got[k : k + nq]]
    bit = 1
    while bit < nb:
        swap = (b & bit) != 0
        blocks = [jnp.where(swap, blocks[i ^ bit], blocks[i]) for i in range(nb)]
        bit *= 2
    s = jnp.concatenate(blocks, axis=0)
    s, doc = s[:, :t], s[:, t:]
    doc = jnp.concatenate([doc, jnp.broadcast_to(count[None, :], doc.shape)], axis=1)

    k = 2
    while k < nb:
        doc = doc + lax.ppermute(doc, "blk", pairs(nb, k))
        k *= 2
    k = nw // 2
    while k:
        half = s.shape[1] // 2
        low = (w & k) == 0
        keep = jnp.where(low, s[:, :half], s[:, half:])
        give = jnp.where(low, s[:, half:], s[:, :half])
        got = lax.ppermute(jnp.concatenate([give, doc], axis=1), "width", pairs(nw, k))
        s = keep + got[:, :half]
        doc = doc + got[:, half:]
        k //= 2
    doc_scores = (doc[:, :docs] / jnp.sqrt(doc[:, docs:])).T
    return (s.T, doc_scores)


def solution(mesh):
    return jax.shard_map(
        per_device,
        mesh=mesh,
        in_specs=(
            P(("groups", "blk"), "width"),
            P(("groups", "blk"), "width", None),
            P(("groups", "blk", "width"), None),
            P(("groups", "blk", "width")),
        ),
        out_specs=(P(("groups", "blk", "width"), None), P("groups", None)),
        check_vma=False,
    )
```

```python
import functools

import jax
import jax.numpy as jnp
from jax import lax
from jax.experimental import pallas as pl
from jax.experimental.pallas import tpu as pltpu
from jax.sharding import PartitionSpec as P

DOC_BLK = 4
LANES = 128
F32, BF16 = jnp.float32, jnp.bfloat16
TILE = 256
LATE = 2
Z_ORDER = 1
MERGE = False
PARTS = (2, 4, 8, 16, 16)
VMEM = pl.BlockSpec(memory_space=pltpu.VMEM)
HBM = pl.BlockSpec(memory_space=pltpu.HBM)
PARAMS = pltpu.CompilerParams(vmem_limit_bytes=16 << 20)
COST = pl.CostEstimate(flops=1, bytes_accessed=1, transcendentals=0)


def split(x):
    high = x.astype(BF16)
    return high, (x - high.astype(F32)).astype(BF16)


def in_hbm(x):
    return pltpu.with_memory_space_constraint(x, pltpu.HBM)


def cut_kernel(pieces, g_ref, *refs):
    outs, sems = refs[:-1], refs[-1]
    copies = [
        pltpu.make_async_copy(g_ref.at[:, at : at + n], out, sems.at[i])
        for i, ((at, n), out) in enumerate(zip(pieces, outs))
    ]
    for copy in copies:
        copy.start()
    for copy in copies:
        copy.wait()


def cut(g, pieces):
    nq, _, r = g.shape
    return pl.pallas_call(
        functools.partial(cut_kernel, pieces),
        in_specs=[HBM],
        out_specs=[VMEM] * len(pieces),
        out_shape=[jax.ShapeDtypeStruct((nq, n, r), F32) for _, n in pieces],
        scratch_shapes=[pltpu.SemaphoreType.DMA((len(pieces),))],
        compiler_params=PARAMS,
        cost_estimate=COST,
    )(in_hbm(g))


def weigh(g_ref, step):
    nq, n, _ = g_ref.shape
    return [
        split(jnp.concatenate([g_ref[q, k : k + step] for q in range(nq)], axis=1))
        for k in range(0, n, step)
    ]


def project(a, weights, step):
    dot = functools.partial(jnp.dot, preferred_element_type=F32)
    p = None
    for i, (gh, gl) in enumerate(weights):
        gh, gl = gh[...], gl[...]
        ah, al = split(a[:, i * step : (i + 1) * step])
        if step < 256:
            part = dot(jnp.concatenate([ah, al, ah], axis=1), jnp.concatenate([gh, gh, gl], axis=0))
        else:
            part = dot(ah, gh) + dot(al, gh) + dot(ah, gl)
        p = part if p is None else p + part
    return p


def contract(p, o):
    r = o.shape[1]
    return [jnp.sum(p[:, q : q + r] * o, axis=1) for q in range(0, p.shape[1], r)]


def score_tile(a, weights, o, step):
    return contract(project(a, weights, step), o)


def project_kernel(staged, a_ref, g_ref, p_ref, stage_ref, high_ref, low_ref):
    step = high_ref.shape[1]
    n = a_ref.shape[1]

    @pl.when(pl.program_id(0) == 0)
    def _():
        for k, (gh, gl) in enumerate(weigh(g_ref, step)):
            high_ref[k] = gh
            low_ref[k] = gl

    a = a_ref[...]
    here = pl.ds(pl.multiple_of(pl.program_id(0) * a.shape[0], a.shape[0]), a.shape[0])
    p_ref[here, :] = project(a, [(high_ref.at[k], low_ref.at[k]) for k in range(n // step)], step)
    stage_ref[here, :] = a[:, n - staged :]


def own_projection(a, g, staged):
    t = a.shape[0]
    nq, n, r = g.shape
    tile, step = min(t, TILE), min(n, 512)
    return pl.pallas_call(
        functools.partial(project_kernel, staged),
        grid=(t // tile,),
        in_specs=[pl.BlockSpec((tile, n), lambda i: (i, 0)), VMEM],
        out_specs=[VMEM, VMEM],
        out_shape=[jax.ShapeDtypeStruct((t, w), F32) for w in (nq * r, staged)],
        scratch_shapes=[pltpu.VMEM((n // step, step, nq * r), BF16)] * 2,
        compiler_params=PARAMS,
        cost_estimate=COST,
    )(in_hbm(a), g)


def near_kernel(staged, a_ref, o_ref, oo_ref, p_ref, g_ref, s_ref, stage_ref, high_ref, low_ref):
    tile, n = a_ref.shape
    t = s_ref.shape[1] // 2
    i = pl.program_id(0)
    step = high_ref.shape[1]

    @pl.when(i == 0)
    def _():
        s_ref[...] = jnp.zeros_like(s_ref)
        for k, (gh, gl) in enumerate(weigh(g_ref, step)):
            high_ref[k] = gh
            low_ref[k] = gl

    a = a_ref[...]
    p = project(a, [(high_ref.at[k], low_ref.at[k]) for k in range(n // step)], step)
    here = pl.ds(pl.multiple_of(i * tile, tile), tile)
    there = pl.ds(pl.multiple_of(t + i * tile, tile), tile)
    for at, p, o in ((here, p_ref[here, :], o_ref[here, :]), (there, p, oo_ref[here, :])):
        for q, row in enumerate(contract(p, o)):
            s_ref[q, at] = row
    stage_ref[here, :] = a[:, n - staged :]


def near_scores(rows, a, outgrads, p, g, staged):
    t = a.shape[0]
    nq, n, r = g.shape
    tile, step = min(t, TILE), min(n, 512)
    return pl.pallas_call(
        functools.partial(near_kernel, staged),
        grid=(t // tile,),
        in_specs=[pl.BlockSpec((tile, n), lambda i: (i, 0)), VMEM, VMEM, VMEM, VMEM],
        out_specs=[VMEM, VMEM],
        out_shape=[jax.ShapeDtypeStruct((rows, 2 * t), F32), jax.ShapeDtypeStruct((t, staged), F32)],
        scratch_shapes=[pltpu.VMEM((n // step, step, nq * r), BF16)] * 2,
        compiler_params=PARAMS,
        cost_estimate=COST,
    )(in_hbm(a), *outgrads, p, g)


def stream_kernel(first, *refs):
    a_refs, o_refs, refs = refs[:2], refs[2:4], refs[4:]
    g_ref, prev_ref, s_ref, high_ref, low_ref = refs
    tile, n = a_refs[0].shape
    t = s_ref.shape[1] // 2
    i = pl.program_id(0)
    step = high_ref.shape[1]

    @pl.when(i == 0)
    def _():
        s_ref[...] = prev_ref[...]
        for k, (gh, gl) in enumerate(weigh(g_ref, step)):
            high_ref[k] = gh
            low_ref[k] = gl

    weights = [(high_ref.at[k], low_ref.at[k]) for k in range(n // step)]
    for h in range(2):
        a = a_refs[h][...]
        at = pl.multiple_of(h * t + i * tile, tile)
        o = o_refs[h][pl.ds(pl.multiple_of(i * tile, tile), tile), :]
        for q, row in enumerate(score_tile(a, weights, o, step)):
            s_ref[first + q, pl.ds(at, tile)] += row


def stream_scores(s, activations, outgrads, g, start, first):
    t = activations[0].shape[0]
    nq, n, r = g.shape
    tile = min(t, 512)
    step = min(n, 512)
    col = start // n
    return pl.pallas_call(
        functools.partial(stream_kernel, first),
        grid=(t // tile,),
        in_specs=[pl.BlockSpec((tile, n), lambda i: (i, col))] * 2
        + [VMEM] * 4,
        out_specs=VMEM,
        out_shape=jax.ShapeDtypeStruct(s.shape, F32),
        scratch_shapes=[pltpu.VMEM((n // step, step, nq * r), BF16)] * 2,
        compiler_params=PARAMS,
        cost_estimate=COST,
    )(*[in_hbm(a) for a in activations], *outgrads, g, s)


def staged_kernel(start, first, *refs):
    a_refs, o_refs, (g_ref, prev_ref, s_ref) = refs[:2], refs[2:4], refs[4:]
    n = g_ref.shape[1]
    t = a_refs[0].shape[0]
    tile = min(t, 256)
    weights = weigh(g_ref, n)
    s_ref[...] = prev_ref[...]
    for h in range(2):
        for m in range(0, t, tile):
            a = a_refs[h][m : m + tile, start : start + n]
            at = h * t + m
            for q, row in enumerate(score_tile(a, weights, o_refs[h][m : m + tile, :], n)):
                s_ref[first + q, at : at + tile] += row


def staged_scores(s, stages, outgrads, g, start, first):
    return pl.pallas_call(
        functools.partial(staged_kernel, start, first),
        in_specs=[VMEM] * 6,
        out_specs=VMEM,
        out_shape=jax.ShapeDtypeStruct(s.shape, F32),
        compiler_params=PARAMS,
        cost_estimate=COST,
    )(*stages, *outgrads, g, s)


def finish_kernel(s_ref, doc_ref, scores_ref, doc_scores_ref):
    docs = doc_scores_ref.shape[1]
    scores_ref[...] = s_ref[...]
    doc = doc_ref[...]
    doc_scores_ref[...] = doc[:, :docs] / jnp.sqrt(doc[:, docs : 2 * docs])


def finish(s, doc, docs):
    return pl.pallas_call(
        finish_kernel,
        in_specs=[VMEM] * 2,
        out_specs=[VMEM] * 2,
        out_shape=[
            jax.ShapeDtypeStruct(s.shape, F32),
            jax.ShapeDtypeStruct((s.shape[0], docs), F32),
        ],
        compiler_params=PARAMS,
        cost_estimate=COST,
    )(s, doc)


def per_device(a, g, o, ids):
    nb, nw = lax.axis_size("blk"), lax.axis_size("width")
    b, w = lax.axis_index("blk"), lax.axis_index("width")
    nq, d, r = g.shape
    t = a.shape[0]
    own = o.shape[0]
    docs = DOC_BLK * nb
    pairs = lambda n, k: [(i, i ^ k) for i in range(n)]
    to_core = lambda x: lax.ppermute(x, "blk", pairs(nb, 1))

    def after(x, *others):
        return lax.optimization_barrier((x, *others))[0]

    pieces, at = [], 0
    for part in PARTS:
        n = max(d // part, LANES)
        if at < d:
            pieces.append((at, n))
        at += n
    cuts = cut(g, pieces[:1])
    ids_other = to_core(ids)
    cuts += cut(after(g, ids_other), pieces[1:])
    sends = [(j, at, x) for j in range(2, nb, 2) for (at, _), x in zip(pieces, cuts)]

    def send(i, *others):
        j, _, x = sends[i]
        return lax.ppermute(after(x, *others), "blk", pairs(nb, j))

    arrived = [send(0), send(1)]
    a_other = to_core(after(a, ids_other))

    rows = own // LANES
    flat = ids.astype(F32).reshape(rows, LANES)
    mine = after(jnp.concatenate([o, flat], axis=0), ids_other)
    late = d - pieces[-LATE][0]
    p, stage = own_projection(a, after(g, ids_other), late)
    table = after(jnp.zeros((t + t // LANES, LANES), F32), p)
    for k in range(nw):
        got = lax.ppermute(mine, "width", pairs(nw, k)) if k else mine
        src = w ^ k
        table = lax.dynamic_update_slice(table, got[:own], (src * own, 0))
        table = lax.dynamic_update_slice(table, got[own:], (t + src * rows, 0))
    other = to_core(table)

    both, outgrads = [a, a_other], [table, other]
    s, stage_other = near_scores(nb // 2 * nq, a_other, outgrads, p, g, late)
    stages = [stage, stage_other]
    arrived.append(send(2, s))
    for i, (j, at, x) in enumerate(sends):
        if i + 3 < len(sends):
            arrived.append(send(i + 3, s))
        first = j // 2 * nq
        if at < d - late:
            s = stream_scores(s, both, outgrads, arrived[i], at, first)
        else:
            s = staged_scores(s, stages, outgrads, arrived[i], at - (d - late), first)

    number = jnp.arange(docs, dtype=F32)
    marks = lambda x: (x.reshape(-1)[:, None] == number[None, :]).astype(F32)
    count = jnp.sum(marks(flat), axis=0) + jnp.sum(marks(ids_other.astype(F32)), axis=0)
    onehot = marks(jnp.concatenate([table[t:], other[t:]], axis=0))
    doc = jnp.dot(s, onehot, precision=lax.Precision.HIGHEST, preferred_element_type=F32)

    keep = jnp.concatenate([s[:, :t], doc], axis=1)
    got = to_core(jnp.concatenate([s[:, t:], doc], axis=1))
    blocks = []
    for k in range(0, nb // 2 * nq, nq):
        blocks += [keep[k : k + nq], got[k : k + nq]]
    bit = 1
    while bit < nb:
        swap = (b & bit) != 0
        blocks = [jnp.where(swap, blocks[i ^ bit], blocks[i]) for i in range(nb)]
        bit *= 2
    s = jnp.concatenate(blocks, axis=0)
    s, doc = s[:, :t], s[:, t:]
    doc = jnp.concatenate([doc, jnp.broadcast_to(count[None, :], doc.shape)], axis=1)

    swap = lambda x, y_bit, z_bit: lax.ppermute(
        x,
        ("blk", "width"),
        [(i * nw + k, (i ^ y_bit) * nw + (k ^ z_bit)) for i in range(nb) for k in range(nw)],
    )
    blocks = {i: s[:, i * own : (i + 1) * own] for i in range(nw)}
    y_bits = [1 << i for i in range(1, nb.bit_length() - 1)]
    z_bits = [1 << i for i in range(nw.bit_length() - 1)][:: Z_ORDER]
    for y_bit in y_bits[:-1]:
        doc = doc + swap(doc, y_bit, 0)
    for z_bit in z_bits:
        low = (w & z_bit) == 0
        at = [i for i in blocks if not i & z_bit]
        give = [jnp.where(low, blocks[i | z_bit], blocks[i]) for i in at]
        keep = [jnp.where(low, blocks[i], blocks[i | z_bit]) for i in at]
        if z_bit == z_bits[0] and MERGE:
            cross, up = swap(doc, y_bits[-1], z_bit), swap(doc, y_bits[-1], 0)
        elif z_bit == z_bits[0]:
            doc = doc + swap(doc, y_bits[-1], 0)
        got = swap(jnp.concatenate(give + [doc], axis=1), 0, z_bit)
        blocks = {i: x + got[:, n * own : (n + 1) * own] for n, (i, x) in enumerate(zip(at, keep))}
        side = got[:, len(at) * own :]
        if z_bit == z_bits[0] and MERGE:
            doc, side = doc + up, side + cross
        doc = doc + side
    scores, doc_scores = finish(blocks[0], doc, docs)
    return (scores.T, doc_scores.T)


def solution(mesh):
    return jax.shard_map(
        per_device,
        mesh=mesh,
        in_specs=(
            P(("groups", "blk"), "width"),
            P(("groups", "blk"), "width", None),
            P(("groups", "blk", "width"), None),
            P(("groups", "blk", "width")),
        ),
        out_specs=(P(("groups", "blk", "width"), None), P("groups", None)),
        check_vma=False,
    )
```

```python
import functools

import jax
import jax.numpy as jnp
from jax import lax
from jax.experimental import pallas as pl
from jax.experimental.pallas import tpu as pltpu
from jax.sharding import PartitionSpec as P

DOC_BLK = 4
LANES = 128
F32, BF16 = jnp.float32, jnp.bfloat16
TILE = 256
Z_ORDER = 1
MERGE = False
PARTS = (2, 4, 8, 16, 16)
VMEM = pl.BlockSpec(memory_space=pltpu.VMEM)
HBM = pl.BlockSpec(memory_space=pltpu.HBM)
PARAMS = pltpu.CompilerParams(vmem_limit_bytes=16 << 20)
COST = pl.CostEstimate(flops=1, bytes_accessed=1, transcendentals=0)


def split(x):
    high = x.astype(BF16)
    return high, (x - high.astype(F32)).astype(BF16)


def in_hbm(x):
    return pltpu.with_memory_space_constraint(x, pltpu.HBM)


def cut_kernel(pieces, g_ref, *refs):
    outs, sems = refs[:-1], refs[-1]
    copies = [
        pltpu.make_async_copy(g_ref.at[:, at : at + n], out, sems.at[i])
        for i, ((at, n), out) in enumerate(zip(pieces, outs))
    ]
    for copy in copies:
        copy.start()
    for copy in copies:
        copy.wait()


def cut(g, pieces):
    nq, _, r = g.shape
    return pl.pallas_call(
        functools.partial(cut_kernel, pieces),
        in_specs=[HBM],
        out_specs=[VMEM] * len(pieces),
        out_shape=[jax.ShapeDtypeStruct((nq, n, r), F32) for _, n in pieces],
        scratch_shapes=[pltpu.SemaphoreType.DMA((len(pieces),))],
        compiler_params=PARAMS,
        cost_estimate=COST,
    )(in_hbm(g))


def weigh(g_ref, step):
    nq, n, _ = g_ref.shape
    return [
        split(jnp.concatenate([g_ref[q, k : k + step] for q in range(nq)], axis=1))
        for k in range(0, n, step)
    ]


def project(a, weights, step):
    dot = functools.partial(jnp.dot, preferred_element_type=F32)
    p = None
    for i, (gh, gl) in enumerate(weights):
        gh, gl = gh[...], gl[...]
        ah, al = split(a[:, i * step : (i + 1) * step])
        if step < 256:
            part = dot(jnp.concatenate([ah, al, ah], axis=1), jnp.concatenate([gh, gh, gl], axis=0))
        else:
            part = dot(ah, gh) + dot(al, gh) + dot(ah, gl)
        p = part if p is None else p + part
    return p


def contract(p, o):
    r = o.shape[1]
    return [jnp.sum(p[:, q : q + r] * o, axis=1) for q in range(0, p.shape[1], r)]


def score_tile(a, weights, o, step):
    return contract(project(a, weights, step), o)


def prepare(g_ref, lead_ref, refs):
    high_ref, low_ref, lead_high_ref, lead_low_ref = refs
    step = high_ref.shape[1]

    @pl.when(pl.program_id(0) == 0)
    def _():
        for k, (gh, gl) in enumerate(weigh(g_ref, step)):
            high_ref[k] = gh
            low_ref[k] = gl
        lead_high_ref[...], lead_low_ref[...] = weigh(lead_ref, lead_ref.shape[1])[0]

    weights = [(high_ref.at[k], low_ref.at[k]) for k in range(high_ref.shape[0])]
    return weights, [(lead_high_ref, lead_low_ref)]


def project_both(a, weights, lead_weights, at):
    step, n = weights[0][0].shape[0], lead_weights[0][0].shape[0]
    return project(a, weights, step), project(a[:, at : at + n], lead_weights, n)


def own_kernel(at, cols, a_ref, g_ref, lead_ref, p_ref, lead_p_ref, stage_ref, *refs):
    weights, lead_weights = prepare(g_ref, lead_ref, refs)
    a = a_ref[...]
    here = pl.ds(pl.multiple_of(pl.program_id(0) * a.shape[0], a.shape[0]), a.shape[0])
    p_ref[here, :], lead_p_ref[here, :] = project_both(a, weights, lead_weights, at)
    stage_ref[here, :] = a[:, cols[0] : cols[1]]


def other_kernel(
    at, cols, a_ref, o_ref, oo_ref, p_ref, lead_p_ref, g_ref, lead_ref, s_ref, stage_ref, *refs
):
    weights, lead_weights = prepare(g_ref, lead_ref, refs)
    a = a_ref[...]
    tile = a.shape[0]
    t = s_ref.shape[1] // 2
    nq = g_ref.shape[0]
    start = pl.program_id(0) * tile

    @pl.when(pl.program_id(0) == 0)
    def _():
        s_ref[...] = jnp.zeros_like(s_ref)

    here = pl.ds(pl.multiple_of(start, tile), tile)
    there = pl.ds(pl.multiple_of(t + start, tile), tile)
    own = p_ref[here, :], lead_p_ref[here, :]
    other = project_both(a, weights, lead_weights, at)
    for to, parts, o in ((here, own, o_ref[here, :]), (there, other, oo_ref[here, :])):
        for i, p in enumerate(parts):
            for q, row in enumerate(contract(p, o)):
                s_ref[i * nq + q, to] = row
    stage_ref[here, :] = a[:, cols[0] : cols[1]]


def near_call(kernel, a, others, g, lead, out):
    t = a.shape[0]
    nq, n, r = g.shape
    tile, step = min(t, TILE), min(n, 512)
    return pl.pallas_call(
        kernel,
        grid=(t // tile,),
        in_specs=[pl.BlockSpec((tile, n), lambda i: (i, 0))] + [VMEM] * (len(others) + 2),
        out_specs=[VMEM] * len(out),
        out_shape=[jax.ShapeDtypeStruct(shape, F32) for shape in out],
        scratch_shapes=[pltpu.VMEM((n // step, step, nq * r), BF16)] * 2
        + [pltpu.VMEM((lead.shape[1], nq * r), BF16)] * 2,
        compiler_params=PARAMS,
        cost_estimate=COST,
    )(in_hbm(a), *others, g, lead)


def stream_kernel(first, *refs):
    a_refs, o_refs, refs = refs[:2], refs[2:4], refs[4:]
    g_ref, prev_ref, s_ref, high_ref, low_ref = refs
    tile, n = a_refs[0].shape
    t = s_ref.shape[1] // 2
    i = pl.program_id(0)
    step = high_ref.shape[1]

    @pl.when(i == 0)
    def _():
        s_ref[...] = prev_ref[...]
        for k, (gh, gl) in enumerate(weigh(g_ref, step)):
            high_ref[k] = gh
            low_ref[k] = gl

    weights = [(high_ref.at[k], low_ref.at[k]) for k in range(n // step)]
    for h in range(2):
        a = a_refs[h][...]
        at = pl.multiple_of(h * t + i * tile, tile)
        o = o_refs[h][pl.ds(pl.multiple_of(i * tile, tile), tile), :]
        for q, row in enumerate(score_tile(a, weights, o, step)):
            s_ref[first + q, pl.ds(at, tile)] += row


def stream_scores(s, activations, outgrads, g, start, first):
    t = activations[0].shape[0]
    nq, n, r = g.shape
    tile = min(t, 512)
    step = min(n, 512)
    col = start // n
    return pl.pallas_call(
        functools.partial(stream_kernel, first),
        grid=(t // tile,),
        in_specs=[pl.BlockSpec((tile, n), lambda i: (i, col))] * 2
        + [VMEM] * 4,
        out_specs=VMEM,
        out_shape=jax.ShapeDtypeStruct(s.shape, F32),
        scratch_shapes=[pltpu.VMEM((n // step, step, nq * r), BF16)] * 2,
        compiler_params=PARAMS,
        cost_estimate=COST,
    )(*[in_hbm(a) for a in activations], *outgrads, g, s)


def staged_kernel(start, first, *refs):
    a_refs, o_refs, (g_ref, prev_ref, s_ref) = refs[:2], refs[2:4], refs[4:]
    n = g_ref.shape[1]
    t = a_refs[0].shape[0]
    tile = min(t, 256)
    weights = weigh(g_ref, n)
    s_ref[...] = prev_ref[...]
    for h in range(2):
        for m in range(0, t, tile):
            a = a_refs[h][m : m + tile, start : start + n]
            at = h * t + m
            for q, row in enumerate(score_tile(a, weights, o_refs[h][m : m + tile, :], n)):
                s_ref[first + q, at : at + tile] += row


def staged_scores(s, stages, outgrads, g, start, first):
    return pl.pallas_call(
        functools.partial(staged_kernel, start, first),
        in_specs=[VMEM] * 6,
        out_specs=VMEM,
        out_shape=jax.ShapeDtypeStruct(s.shape, F32),
        compiler_params=PARAMS,
        cost_estimate=COST,
    )(*stages, *outgrads, g, s)


def finish_kernel(s_ref, doc_ref, scores_ref, doc_scores_ref):
    docs = doc_scores_ref.shape[1]
    scores_ref[...] = s_ref[...]
    doc = doc_ref[...]
    doc_scores_ref[...] = doc[:, :docs] / jnp.sqrt(doc[:, docs : 2 * docs])


def finish(s, doc, docs):
    return pl.pallas_call(
        finish_kernel,
        in_specs=[VMEM] * 2,
        out_specs=[VMEM] * 2,
        out_shape=[
            jax.ShapeDtypeStruct(s.shape, F32),
            jax.ShapeDtypeStruct((s.shape[0], docs), F32),
        ],
        compiler_params=PARAMS,
        cost_estimate=COST,
    )(s, doc)


def per_device(a, g, o, ids):
    nb, nw = lax.axis_size("blk"), lax.axis_size("width")
    b, w = lax.axis_index("blk"), lax.axis_index("width")
    nq, d, r = g.shape
    t = a.shape[0]
    own = o.shape[0]
    docs = DOC_BLK * nb
    pairs = lambda n, k: [(i, i ^ k) for i in range(n)]
    to_core = lambda x: lax.ppermute(x, "blk", pairs(nb, 1))

    def after(x, *others):
        return lax.optimization_barrier((x, *others))[0]

    pieces, at = [], 0
    for part in PARTS:
        n = max(d // part, LANES)
        if at < d:
            pieces.append((at, n))
        at += n
    pieces = pieces[-1:] + pieces[:-1]
    cuts = cut(g, pieces[:1])
    lead = lax.ppermute(cuts[0], "blk", pairs(nb, 2))
    cuts += cut(after(g, cuts[0]), pieces[1:2])
    a_other = to_core(after(a, cuts[0]))
    cuts += cut(after(g, lead), pieces[2:])
    at, last = pieces[0][0], pieces[-1]
    cols = last[0], sum(last)
    wide = (t, nq * r), (t, nq * r), (t, last[1])
    a_own = after(a, lead, *cuts[2:])
    p, lead_p, stage = near_call(functools.partial(own_kernel, at, cols), a_own, [], g, lead, wide)
    sends = [(j, at, x) for j in range(2, nb, 2) for (at, _), x in zip(pieces, cuts)]

    def send(i, *others):
        j, _, x = sends[i]
        return lax.ppermute(after(x, *others), "blk", pairs(nb, j))

    arrived = [lead, lax.ppermute(cuts[1], "blk", pairs(nb, 2)), send(2, lead)]

    rows = own // LANES
    flat = ids.astype(F32).reshape(rows, LANES)
    mine = after(jnp.concatenate([o, flat], axis=0), lead)
    table = after(jnp.zeros((t + t // LANES, LANES), F32), p)
    for k in range(nw):
        got = lax.ppermute(mine, "width", pairs(nw, k)) if k else mine
        src = w ^ k
        table = lax.dynamic_update_slice(table, got[:own], (src * own, 0))
        table = lax.dynamic_update_slice(table, got[own:], (t + src * rows, 0))
    other = to_core(table)

    both, outgrads = [a, a_other], [table, other]
    s, stage_other = near_call(
        functools.partial(other_kernel, at, cols),
        a_other,
        [*outgrads, p, lead_p],
        g,
        lead,
        ((nb // 2 * nq, 2 * t), wide[2]),
    )
    stages = [stage, stage_other]
    arrived.append(send(3, s))
    for i, (j, at, x) in enumerate(sends):
        if i + 4 < len(sends):
            arrived.append(send(i + 4, s))
        first = j // 2 * nq
        if i == 0:
            continue
        if at == last[0]:
            s = staged_scores(s, stages, outgrads, arrived[i], 0, first)
        else:
            s = stream_scores(s, both, outgrads, arrived[i], at, first)

    number = jnp.arange(docs, dtype=F32)
    marks = lambda x: (x.reshape(-1)[:, None] == number[None, :]).astype(F32)
    onehot = marks(jnp.concatenate([table[t:], other[t:]], axis=0))
    count = jnp.sum(onehot, axis=0) / nw
    doc = jnp.dot(s, onehot, precision=lax.Precision.HIGHEST, preferred_element_type=F32)

    keep = jnp.concatenate([s[:, :t], doc], axis=1)
    got = to_core(jnp.concatenate([s[:, t:], doc], axis=1))
    blocks = []
    for k in range(0, nb // 2 * nq, nq):
        blocks += [keep[k : k + nq], got[k : k + nq]]
    bit = 1
    while bit < nb:
        swap = (b & bit) != 0
        blocks = [jnp.where(swap, blocks[i ^ bit], blocks[i]) for i in range(nb)]
        bit *= 2
    s = jnp.concatenate(blocks, axis=0)
    s, doc = s[:, :t], s[:, t:]
    doc = jnp.concatenate([doc, jnp.broadcast_to(count[None, :], doc.shape)], axis=1)

    swap = lambda x, y_bit, z_bit: lax.ppermute(
        x,
        ("blk", "width"),
        [(i * nw + k, (i ^ y_bit) * nw + (k ^ z_bit)) for i in range(nb) for k in range(nw)],
    )
    blocks = {i: s[:, i * own : (i + 1) * own] for i in range(nw)}
    y_bits = [1 << i for i in range(1, nb.bit_length() - 1)]
    z_bits = [1 << i for i in range(nw.bit_length() - 1)][:: Z_ORDER]
    for y_bit in y_bits[:-1]:
        doc = doc + swap(doc, y_bit, 0)
    for z_bit in z_bits:
        low = (w & z_bit) == 0
        at = [i for i in blocks if not i & z_bit]
        give = [jnp.where(low, blocks[i | z_bit], blocks[i]) for i in at]
        keep = [jnp.where(low, blocks[i], blocks[i | z_bit]) for i in at]
        if z_bit == z_bits[0] and MERGE:
            cross, up = swap(doc, y_bits[-1], z_bit), swap(doc, y_bits[-1], 0)
        elif z_bit == z_bits[0]:
            doc = doc + swap(doc, y_bits[-1], 0)
        got = swap(jnp.concatenate(give + [doc], axis=1), 0, z_bit)
        blocks = {i: x + got[:, n * own : (n + 1) * own] for n, (i, x) in enumerate(zip(at, keep))}
        side = got[:, len(at) * own :]
        if z_bit == z_bits[0] and MERGE:
            doc, side = doc + up, side + cross
        doc = doc + side
    scores, doc_scores = finish(blocks[0], doc, docs)
    return (scores.T, doc_scores.T)


def solution(mesh):
    return jax.shard_map(
        per_device,
        mesh=mesh,
        in_specs=(
            P(("groups", "blk"), "width"),
            P(("groups", "blk"), "width", None),
            P(("groups", "blk", "width"), None),
            P(("groups", "blk", "width")),
        ),
        out_specs=(P(("groups", "blk", "width"), None), P("groups", None)),
        check_vma=False,
    )
```

```python
import functools

import jax
import jax.numpy as jnp
from jax import lax
from jax.experimental import pallas as pl
from jax.experimental.pallas import tpu as pltpu
from jax.sharding import PartitionSpec as P

DOC_BLK = 4
LANES = 128
F32, BF16 = jnp.float32, jnp.bfloat16
TILE = 256
PARTS = (2, 4, 8, 16, 16)
VMEM = pl.BlockSpec(memory_space=pltpu.VMEM)
HBM = pl.BlockSpec(memory_space=pltpu.HBM)
PARAMS = pltpu.CompilerParams(vmem_limit_bytes=16 << 20)
COST = pl.CostEstimate(flops=1, bytes_accessed=1, transcendentals=0)


def split(x):
    high = x.astype(BF16)
    return high, (x - high.astype(F32)).astype(BF16)


def in_hbm(x):
    return pltpu.with_memory_space_constraint(x, pltpu.HBM)


def cut_kernel(pieces, g_ref, *refs):
    outs, sems = refs[:-1], refs[-1]
    copies = [
        pltpu.make_async_copy(g_ref.at[:, at : at + n], out, sems.at[i])
        for i, ((at, n), out) in enumerate(zip(pieces, outs))
    ]
    for copy in copies:
        copy.start()
    for copy in copies:
        copy.wait()


def cut(g, pieces):
    nq, _, r = g.shape
    return pl.pallas_call(
        functools.partial(cut_kernel, pieces),
        in_specs=[HBM],
        out_specs=[VMEM] * len(pieces),
        out_shape=[jax.ShapeDtypeStruct((nq, n, r), F32) for _, n in pieces],
        scratch_shapes=[pltpu.SemaphoreType.DMA((len(pieces),))],
        compiler_params=PARAMS,
        cost_estimate=COST,
    )(in_hbm(g))


def weigh(g_ref, step):
    nq, n, _ = g_ref.shape
    return [
        split(jnp.concatenate([g_ref[q, k : k + step] for q in range(nq)], axis=1))
        for k in range(0, n, step)
    ]


def project(a, weights, step):
    dot = functools.partial(jnp.dot, preferred_element_type=F32)
    p = None
    for i, (gh, gl) in enumerate(weights):
        gh, gl = gh[...], gl[...]
        ah, al = split(a[:, i * step : (i + 1) * step])
        if step < 256:
            part = dot(jnp.concatenate([ah, al, ah], axis=1), jnp.concatenate([gh, gh, gl], axis=0))
        else:
            part = dot(ah, gh) + dot(al, gh) + dot(ah, gl)
        p = part if p is None else p + part
    return p


def contract(p, o):
    r = o.shape[1]
    return [jnp.sum(p[:, q : q + r] * o, axis=1) for q in range(0, p.shape[1], r)]


def score_tile(a, weights, o, step):
    return contract(project(a, weights, step), o)


def prepare(g_ref, lead_ref, refs):
    high_ref, low_ref, lead_high_ref, lead_low_ref = refs
    step = high_ref.shape[1]

    @pl.when(pl.program_id(0) == 0)
    def _():
        for k, (gh, gl) in enumerate(weigh(g_ref, step)):
            high_ref[k] = gh
            low_ref[k] = gl
        lead_high_ref[...], lead_low_ref[...] = weigh(lead_ref, lead_ref.shape[1])[0]

    weights = [(high_ref.at[k], low_ref.at[k]) for k in range(high_ref.shape[0])]
    return weights, [(lead_high_ref, lead_low_ref)]


def project_both(a, weights, lead_weights, at):
    step, n = weights[0][0].shape[0], lead_weights[0][0].shape[0]
    return project(a, weights, step), project(a[:, at : at + n], lead_weights, n)


def own_kernel(at, cols, a_ref, g_ref, lead_ref, p_ref, lead_p_ref, stage_ref, *refs):
    weights, lead_weights = prepare(g_ref, lead_ref, refs)
    a = a_ref[...]
    here = pl.ds(pl.multiple_of(pl.program_id(0) * a.shape[0], a.shape[0]), a.shape[0])
    p_ref[here, :], lead_p_ref[here, :] = project_both(a, weights, lead_weights, at)
    stage_ref[here, :] = a[:, cols[0] : cols[1]]


def other_kernel(
    at, cols, a_ref, o_ref, oo_ref, p_ref, lead_p_ref, g_ref, lead_ref, s_ref, stage_ref, *refs
):
    weights, lead_weights = prepare(g_ref, lead_ref, refs)
    a = a_ref[...]
    tile = a.shape[0]
    t = s_ref.shape[1] // 2
    nq = g_ref.shape[0]
    start = pl.program_id(0) * tile

    @pl.when(pl.program_id(0) == 0)
    def _():
        s_ref[...] = jnp.zeros_like(s_ref)

    here = pl.ds(pl.multiple_of(start, tile), tile)
    there = pl.ds(pl.multiple_of(t + start, tile), tile)
    own = p_ref[here, :], lead_p_ref[here, :]
    other = project_both(a, weights, lead_weights, at)
    for to, parts, o in ((here, own, o_ref[here, :]), (there, other, oo_ref[here, :])):
        for i, p in enumerate(parts):
            for q, row in enumerate(contract(p, o)):
                s_ref[i * nq + q, to] = row
    stage_ref[here, :] = a[:, cols[0] : cols[1]]


def near_call(kernel, a, others, g, lead, out):
    t = a.shape[0]
    nq, n, r = g.shape
    tile, step = min(t, TILE), min(n, 512)
    return pl.pallas_call(
        kernel,
        grid=(t // tile,),
        in_specs=[pl.BlockSpec((tile, n), lambda i: (i, 0))] + [VMEM] * (len(others) + 2),
        out_specs=[VMEM] * len(out),
        out_shape=[jax.ShapeDtypeStruct(shape, F32) for shape in out],
        scratch_shapes=[pltpu.VMEM((n // step, step, nq * r), BF16)] * 2
        + [pltpu.VMEM((lead.shape[1], nq * r), BF16)] * 2,
        compiler_params=PARAMS,
        cost_estimate=COST,
    )(in_hbm(a), *others, g, lead)


def stream_kernel(first, *refs):
    a_refs, o_refs, refs = refs[:2], refs[2:4], refs[4:]
    g_ref, prev_ref, s_ref, high_ref, low_ref = refs
    tile, n = a_refs[0].shape
    t = s_ref.shape[1] // 2
    i = pl.program_id(0)
    step = high_ref.shape[1]

    @pl.when(i == 0)
    def _():
        s_ref[...] = prev_ref[...]
        for k, (gh, gl) in enumerate(weigh(g_ref, step)):
            high_ref[k] = gh
            low_ref[k] = gl

    weights = [(high_ref.at[k], low_ref.at[k]) for k in range(n // step)]
    for h in range(2):
        a = a_refs[h][...]
        at = pl.multiple_of(h * t + i * tile, tile)
        o = o_refs[h][pl.ds(pl.multiple_of(i * tile, tile), tile), :]
        for q, row in enumerate(score_tile(a, weights, o, step)):
            s_ref[first + q, pl.ds(at, tile)] += row


def stream_scores(s, activations, outgrads, g, start, first):
    t = activations[0].shape[0]
    nq, n, r = g.shape
    tile = min(t, 512)
    step = min(n, 512)
    col = start // n
    return pl.pallas_call(
        functools.partial(stream_kernel, first),
        grid=(t // tile,),
        in_specs=[pl.BlockSpec((tile, n), lambda i: (i, col))] * 2
        + [VMEM] * 4,
        out_specs=VMEM,
        out_shape=jax.ShapeDtypeStruct(s.shape, F32),
        scratch_shapes=[pltpu.VMEM((n // step, step, nq * r), BF16)] * 2,
        compiler_params=PARAMS,
        cost_estimate=COST,
    )(*[in_hbm(a) for a in activations], *outgrads, g, s)


def staged_kernel(start, first, *refs):
    a_refs, o_refs, (g_ref, prev_ref, s_ref) = refs[:2], refs[2:4], refs[4:]
    n = g_ref.shape[1]
    t = a_refs[0].shape[0]
    tile = min(t, 256)
    weights = weigh(g_ref, n)
    s_ref[...] = prev_ref[...]
    for h in range(2):
        for m in range(0, t, tile):
            a = a_refs[h][m : m + tile, start : start + n]
            at = h * t + m
            for q, row in enumerate(score_tile(a, weights, o_refs[h][m : m + tile, :], n)):
                s_ref[first + q, at : at + tile] += row


def staged_scores(s, stages, outgrads, g, start, first):
    return pl.pallas_call(
        functools.partial(staged_kernel, start, first),
        in_specs=[VMEM] * 6,
        out_specs=VMEM,
        out_shape=jax.ShapeDtypeStruct(s.shape, F32),
        compiler_params=PARAMS,
        cost_estimate=COST,
    )(*stages, *outgrads, g, s)


def finish_kernel(s_ref, doc_ref, scores_ref, doc_scores_ref):
    docs = doc_scores_ref.shape[1]
    scores_ref[...] = s_ref[...]
    doc = doc_ref[...]
    doc_scores_ref[...] = doc[:, :docs] / jnp.sqrt(doc[:, docs : 2 * docs])


def finish(s, doc, docs):
    return pl.pallas_call(
        finish_kernel,
        in_specs=[VMEM] * 2,
        out_specs=[VMEM] * 2,
        out_shape=[
            jax.ShapeDtypeStruct(s.shape, F32),
            jax.ShapeDtypeStruct((s.shape[0], docs), F32),
        ],
        compiler_params=PARAMS,
        cost_estimate=COST,
    )(s, doc)


def per_device(a, g, o, ids):
    nb, nw = lax.axis_size("blk"), lax.axis_size("width")
    b, w = lax.axis_index("blk"), lax.axis_index("width")
    nq, d, r = g.shape
    t = a.shape[0]
    own = o.shape[0]
    docs = DOC_BLK * nb
    pairs = lambda n, k: [(i, i ^ k) for i in range(n)]
    to_core = lambda x: lax.ppermute(x, "blk", pairs(nb, 1))

    def after(x, *others):
        return lax.optimization_barrier((x, *others))[0]

    pieces, at = [], 0
    for part in PARTS:
        n = max(d // part, LANES)
        if at < d:
            pieces.append((at, n))
        at += n
    pieces = pieces[-1:] + pieces[:-1]
    cuts = cut(g, pieces[:1])
    lead = lax.ppermute(cuts[0], "blk", pairs(nb, 2))
    cuts += cut(after(g, cuts[0]), pieces[1:2])
    a_other = to_core(after(a, cuts[0]))
    cuts += cut(after(g, lead), pieces[2:])
    at, last = pieces[0][0], pieces[-1]
    cols = pieces[-2][0], sum(last)
    wide = (t, nq * r), (t, nq * r), (t, cols[1] - cols[0])
    a_own = after(a, lead, *cuts[2:])
    p, lead_p, stage = near_call(functools.partial(own_kernel, at, cols), a_own, [], g, lead, wide)
    sends = [(j, at, x) for j in range(2, nb, 2) for (at, _), x in zip(pieces, cuts)]

    def send(i, *others):
        j, _, x = sends[i]
        return lax.ppermute(after(x, *others), "blk", pairs(nb, j))

    arrived = [lead, lax.ppermute(cuts[1], "blk", pairs(nb, 2)), send(2, lead)]

    rows = own // LANES
    flat = ids.astype(F32).reshape(rows, LANES)
    mine = after(jnp.concatenate([o, flat], axis=0), lead)
    table = after(jnp.zeros((t + t // LANES, LANES), F32), p)
    for k in range(nw):
        got = lax.ppermute(mine, "width", pairs(nw, k)) if k else mine
        src = w ^ k
        table = lax.dynamic_update_slice(table, got[:own], (src * own, 0))
        table = lax.dynamic_update_slice(table, got[own:], (t + src * rows, 0))
    other = to_core(table)

    both, outgrads = [a, a_other], [table, other]
    s, stage_other = near_call(
        functools.partial(other_kernel, at, cols),
        a_other,
        [*outgrads, p, lead_p],
        g,
        lead,
        ((nb // 2 * nq, 2 * t), wide[2]),
    )
    stages = [stage, stage_other]
    arrived.append(send(3, s))
    for i, (j, at, x) in enumerate(sends):
        if i + 4 < len(sends):
            arrived.append(send(i + 4, s))
        first = j // 2 * nq
        if i == 0:
            continue
        if cols[0] <= at < cols[1]:
            s = staged_scores(s, stages, outgrads, arrived[i], at - cols[0], first)
        else:
            s = stream_scores(s, both, outgrads, arrived[i], at, first)

    number = jnp.arange(docs, dtype=F32)
    marks = lambda x: (x.reshape(-1)[:, None] == number[None, :]).astype(F32)
    onehot = marks(jnp.concatenate([table[t:], other[t:]], axis=0))
    count = jnp.sum(onehot, axis=0) / nw
    doc = jnp.dot(s, onehot, precision=lax.Precision.HIGHEST, preferred_element_type=F32)

    keep = jnp.concatenate([s[:, :t], doc], axis=1)
    got = to_core(jnp.concatenate([s[:, t:], doc], axis=1))
    blocks = []
    for k in range(0, nb // 2 * nq, nq):
        blocks += [keep[k : k + nq], got[k : k + nq]]
    bit = 1
    while bit < nb:
        swap = (b & bit) != 0
        blocks = [jnp.where(swap, blocks[i ^ bit], blocks[i]) for i in range(nb)]
        bit *= 2
    s = jnp.concatenate(blocks, axis=0)
    s, doc = s[:, :t], s[:, t:]
    doc = jnp.concatenate([doc, jnp.broadcast_to(count[None, :], doc.shape)], axis=1)

    swap = lambda x, y_bit, z_bit: lax.ppermute(
        x,
        ("blk", "width"),
        [(i * nw + k, (i ^ y_bit) * nw + (k ^ z_bit)) for i in range(nb) for k in range(nw)],
    )
    blocks = {i: s[:, i * own : (i + 1) * own] for i in range(nw)}
    y_bits = [1 << i for i in range(1, nb.bit_length() - 1)]
    z_bits = [1 << i for i in range(nw.bit_length() - 1)]
    for y_bit in y_bits[:-1]:
        doc = doc + swap(doc, y_bit, 0)
    for z_bit in z_bits:
        low = (w & z_bit) == 0
        at = [i for i in blocks if not i & z_bit]
        give = [jnp.where(low, blocks[i | z_bit], blocks[i]) for i in at]
        keep = [jnp.where(low, blocks[i], blocks[i | z_bit]) for i in at]
        if z_bit == z_bits[0]:
            cross, up = swap(doc, y_bits[-1], z_bit), swap(doc, y_bits[-1], 0)
        got = swap(jnp.concatenate(give + [doc], axis=1), 0, z_bit)
        blocks = {i: x + got[:, n * own : (n + 1) * own] for n, (i, x) in enumerate(zip(at, keep))}
        side = got[:, len(at) * own :]
        if z_bit == z_bits[0]:
            doc, side = doc + up, side + cross
        doc = doc + side
    scores, doc_scores = finish(blocks[0], doc, docs)
    return (scores.T, doc_scores.T)


def solution(mesh):
    return jax.shard_map(
        per_device,
        mesh=mesh,
        in_specs=(
            P(("groups", "blk"), "width"),
            P(("groups", "blk"), "width", None),
            P(("groups", "blk", "width"), None),
            P(("groups", "blk", "width")),
        ),
        out_specs=(P(("groups", "blk", "width"), None), P("groups", None)),
        check_vma=False,
    )
```

```python
import functools

import jax
import jax.numpy as jnp
from jax import lax
from jax.experimental import pallas as pl
from jax.experimental.pallas import tpu as pltpu
from jax.sharding import PartitionSpec as P

DOC_BLK = 4
LANES = 128
F32, BF16 = jnp.float32, jnp.bfloat16
TILE = 256
LEADS = 1
PARTS = (2, 4, 8, 16, 16)
VMEM = pl.BlockSpec(memory_space=pltpu.VMEM)
HBM = pl.BlockSpec(memory_space=pltpu.HBM)
PARAMS = pltpu.CompilerParams(vmem_limit_bytes=16 << 20)
COST = pl.CostEstimate(flops=1, bytes_accessed=1, transcendentals=0)


def split(x):
    high = x.astype(BF16)
    return high, (x - high.astype(F32)).astype(BF16)


def in_hbm(x):
    return pltpu.with_memory_space_constraint(x, pltpu.HBM)


def cut_kernel(pieces, g_ref, *refs):
    outs, sems = refs[:-1], refs[-1]
    copies = [
        pltpu.make_async_copy(g_ref.at[:, at : at + n], out, sems.at[i])
        for i, ((at, n), out) in enumerate(zip(pieces, outs))
    ]
    for copy in copies:
        copy.start()
    for copy in copies:
        copy.wait()


def cut(g, pieces):
    nq, _, r = g.shape
    return pl.pallas_call(
        functools.partial(cut_kernel, pieces),
        in_specs=[HBM],
        out_specs=[VMEM] * len(pieces),
        out_shape=[jax.ShapeDtypeStruct((nq, n, r), F32) for _, n in pieces],
        scratch_shapes=[pltpu.SemaphoreType.DMA((len(pieces),))],
        compiler_params=PARAMS,
        cost_estimate=COST,
    )(in_hbm(g))


def weigh(g_ref, step):
    nq, n, _ = g_ref.shape
    return [
        split(jnp.concatenate([g_ref[q, k : k + step] for q in range(nq)], axis=1))
        for k in range(0, n, step)
    ]


def project(a, weights, step):
    dot = functools.partial(jnp.dot, preferred_element_type=F32)
    p = None
    for i, (gh, gl) in enumerate(weights):
        gh, gl = gh[...], gl[...]
        ah, al = split(a[:, i * step : (i + 1) * step])
        if step < 256:
            part = dot(jnp.concatenate([ah, al, ah], axis=1), jnp.concatenate([gh, gh, gl], axis=0))
        else:
            part = dot(ah, gh) + dot(al, gh) + dot(ah, gl)
        p = part if p is None else p + part
    return p


def contract(p, o):
    r = o.shape[1]
    return [jnp.sum(p[:, q : q + r] * o, axis=1) for q in range(0, p.shape[1], r)]


def score_tile(a, weights, o, step):
    return contract(project(a, weights, step), o)


def prepare(g_ref, lead_refs, refs):
    high_ref, low_ref, lead_high_ref, lead_low_ref = refs
    step = high_ref.shape[1]

    @pl.when(pl.program_id(0) == 0)
    def _():
        for k, (gh, gl) in enumerate(weigh(g_ref, step)):
            high_ref[k] = gh
            low_ref[k] = gl
        for k, lead_ref in enumerate(lead_refs):
            lead_high_ref[k], lead_low_ref[k] = weigh(lead_ref, lead_ref.shape[1])[0]

    weights = [(high_ref.at[k], low_ref.at[k]) for k in range(high_ref.shape[0])]
    return weights, [(lead_high_ref.at[k], lead_low_ref.at[k]) for k in range(LEADS)]


def project_both(a, weights, lead_weights, at):
    step, n = weights[0][0].shape[0], lead_weights[0][0].shape[0]
    lead_p = project(a[:, at : at + LEADS * n], lead_weights, n)
    return project(a, weights, step), lead_p


def own_kernel(at, cols, a_ref, g_ref, *refs):
    lead_refs, (p_ref, stage_ref, *refs) = refs[:LEADS], refs[LEADS:]
    weights, lead_weights = prepare(g_ref, lead_refs, refs)
    a = a_ref[...]
    p_ref[...] = jnp.concatenate(project_both(a, weights, lead_weights, at), axis=1)
    stage_ref[...] = a[:, cols[0] : cols[1]]


def other_kernel(at, cols, a_ref, p_ref, o_ref, oo_ref, g_ref, *refs):
    lead_refs, (s_ref, stage_ref, *refs) = refs[:LEADS], refs[LEADS:]
    weights, lead_weights = prepare(g_ref, lead_refs, refs)
    a = a_ref[...]
    tile = a.shape[0]
    t = s_ref.shape[1] // 2
    nq = g_ref.shape[0]
    start = pl.program_id(0) * tile

    @pl.when(pl.program_id(0) == 0)
    def _():
        s_ref[...] = jnp.zeros_like(s_ref)

    here = pl.ds(pl.multiple_of(start, tile), tile)
    there = pl.ds(pl.multiple_of(t + start, tile), tile)
    own = jnp.split(p_ref[...], 2, axis=1)
    other = project_both(a, weights, lead_weights, at)
    for to, parts, o in ((here, own, o_ref[here, :]), (there, other, oo_ref[here, :])):
        for i, p in enumerate(parts):
            for q, row in enumerate(contract(p, o)):
                s_ref[i * nq + q, to] = row
    stage_ref[...] = a[:, cols[0] : cols[1]]


def near_call(kernel, tiled, others, g, leads, whole_out, tiled_out):
    t, n = tiled[0].shape
    nq, _, r = g.shape
    tile, step = min(t, TILE), min(n, 512)
    tiles = lambda width: pl.BlockSpec((tile, width), lambda i: (i, 0))
    return pl.pallas_call(
        kernel,
        grid=(t // tile,),
        in_specs=[tiles(x.shape[1]) for x in tiled] + [VMEM] * (len(others) + 1 + LEADS),
        out_specs=[VMEM] * len(whole_out) + [tiles(width) for width in tiled_out],
        out_shape=[jax.ShapeDtypeStruct(shape, F32) for shape in whole_out]
        + [pltpu.HBM((t, width), F32) for width in tiled_out],
        scratch_shapes=[pltpu.VMEM((n // step, step, nq * r), BF16)] * 2
        + [pltpu.VMEM((LEADS, leads[0].shape[1], nq * r), BF16)] * 2,
        compiler_params=PARAMS,
        cost_estimate=COST,
    )(*[in_hbm(x) for x in tiled], *others, g, *leads)


def stream_kernel(first, *refs):
    a_refs, o_refs, refs = refs[:2], refs[2:4], refs[4:]
    g_ref, prev_ref, s_ref, high_ref, low_ref = refs
    tile, n = a_refs[0].shape
    t = s_ref.shape[1] // 2
    i = pl.program_id(0)
    step = high_ref.shape[1]

    @pl.when(i == 0)
    def _():
        s_ref[...] = prev_ref[...]
        for k, (gh, gl) in enumerate(weigh(g_ref, step)):
            high_ref[k] = gh
            low_ref[k] = gl

    weights = [(high_ref.at[k], low_ref.at[k]) for k in range(n // step)]
    for h in range(2):
        a = a_refs[h][...]
        at = pl.multiple_of(h * t + i * tile, tile)
        o = o_refs[h][pl.ds(pl.multiple_of(i * tile, tile), tile), :]
        for q, row in enumerate(score_tile(a, weights, o, step)):
            s_ref[first + q, pl.ds(at, tile)] += row


def stream_scores(s, activations, outgrads, g, start, first):
    t = activations[0].shape[0]
    nq, n, r = g.shape
    tile = min(t, 512)
    step = min(n, 512)
    col = start // n
    return pl.pallas_call(
        functools.partial(stream_kernel, first),
        grid=(t // tile,),
        in_specs=[pl.BlockSpec((tile, n), lambda i: (i, col))] * 2
        + [VMEM] * 4,
        out_specs=VMEM,
        out_shape=jax.ShapeDtypeStruct(s.shape, F32),
        scratch_shapes=[pltpu.VMEM((n // step, step, nq * r), BF16)] * 2,
        compiler_params=PARAMS,
        cost_estimate=COST,
    )(*[in_hbm(a) for a in activations], *outgrads, g, s)


def staged_kernel(start, first, *refs):
    a_refs, o_refs, (g_ref, prev_ref, s_ref) = refs[:2], refs[2:4], refs[4:]
    n = g_ref.shape[1]
    t = a_refs[0].shape[0]
    tile = min(t, 256)
    weights = weigh(g_ref, n)
    s_ref[...] = prev_ref[...]
    for h in range(2):
        for m in range(0, t, tile):
            a = a_refs[h][m : m + tile, start : start + n]
            at = h * t + m
            for q, row in enumerate(score_tile(a, weights, o_refs[h][m : m + tile, :], n)):
                s_ref[first + q, at : at + tile] += row


def staged_scores(s, stages, outgrads, g, start, first):
    return pl.pallas_call(
        functools.partial(staged_kernel, start, first),
        in_specs=[VMEM] * 6,
        out_specs=VMEM,
        out_shape=jax.ShapeDtypeStruct(s.shape, F32),
        compiler_params=PARAMS,
        cost_estimate=COST,
    )(*stages, *outgrads, g, s)


def finish_kernel(s_ref, doc_ref, scores_ref, doc_scores_ref):
    docs = doc_scores_ref.shape[1]
    scores_ref[...] = s_ref[...]
    doc = doc_ref[...]
    doc_scores_ref[...] = doc[:, :docs] / jnp.sqrt(doc[:, docs : 2 * docs])


def finish(s, doc, docs):
    return pl.pallas_call(
        finish_kernel,
        in_specs=[VMEM] * 2,
        out_specs=[VMEM] * 2,
        out_shape=[
            jax.ShapeDtypeStruct(s.shape, F32),
            jax.ShapeDtypeStruct((s.shape[0], docs), F32),
        ],
        compiler_params=PARAMS,
        cost_estimate=COST,
    )(s, doc)


def per_device(a, g, o, ids):
    nb, nw = lax.axis_size("blk"), lax.axis_size("width")
    b, w = lax.axis_index("blk"), lax.axis_index("width")
    nq, d, r = g.shape
    t = a.shape[0]
    own = o.shape[0]
    docs = DOC_BLK * nb
    pairs = lambda n, k: [(i, i ^ k) for i in range(n)]
    to_core = lambda x: lax.ppermute(x, "blk", pairs(nb, 1))

    def after(x, *others):
        return lax.optimization_barrier((x, *others))[0]

    pieces, at = [], 0
    for part in PARTS:
        n = max(d // part, LANES)
        if at < d:
            pieces.append((at, n))
        at += n
    pieces = pieces[-LEADS:] + pieces[:-LEADS]
    cuts = [g[:, at : at + n] for at, n in pieces[:LEADS]]
    leads = [lax.ppermute(x, "blk", pairs(nb, 2)) for x in cuts]
    lead = leads[0]
    cuts += cut(after(g, cuts[0]), pieces[LEADS : LEADS + 1])
    a_other = to_core(after(a, cuts[0]))
    cuts += cut(after(g, lead), pieces[LEADS + 1 :])
    at = pieces[0][0]
    cols = min(i for i, n in pieces if n <= 512 and i < at), at
    a_own = after(a, lead, *cuts[LEADS + 1 :])
    p, stage = near_call(
        functools.partial(own_kernel, at, cols),
        [a_own],
        [],
        g,
        leads,
        [],
        [2 * nq * r, cols[1] - cols[0]],
    )
    sends = [(j, at, x) for j in range(2, nb, 2) for (at, _), x in zip(pieces, cuts)]

    def send(i, *others):
        j, _, x = sends[i]
        return lax.ppermute(after(x, *others), "blk", pairs(nb, j))

    arrived = leads + [lax.ppermute(cuts[LEADS], "blk", pairs(nb, 2)), send(LEADS + 1, lead)]

    rows = own // LANES
    flat = ids.astype(F32).reshape(rows, LANES)
    mine = after(jnp.concatenate([o, flat], axis=0), lead)
    table = after(jnp.zeros((t + t // LANES, LANES), F32), p)
    for k in range(nw):
        got = lax.ppermute(mine, "width", pairs(nw, k)) if k else mine
        src = w ^ k
        table = lax.dynamic_update_slice(table, got[:own], (src * own, 0))
        table = lax.dynamic_update_slice(table, got[own:], (t + src * rows, 0))
    other = to_core(table)

    both, outgrads = [a, a_other], [table, other]
    s, stage_other = near_call(
        functools.partial(other_kernel, at, cols),
        [a_other, p],
        outgrads,
        g,
        leads,
        [(nb // 2 * nq, 2 * t)],
        [cols[1] - cols[0]],
    )
    stages = [stage, stage_other]
    arrived.append(send(LEADS + 2, s))
    for i, (j, at, x) in enumerate(sends):
        if i + LEADS + 3 < len(sends):
            arrived.append(send(i + LEADS + 3, s))
        first = j // 2 * nq
        if i < LEADS:
            continue
        if cols[0] <= at < cols[1]:
            s = staged_scores(s, stages, outgrads, arrived[i], at - cols[0], first)
        else:
            s = stream_scores(s, both, outgrads, arrived[i], at, first)

    number = jnp.arange(docs, dtype=F32)
    marks = lambda x: (x.reshape(-1)[:, None] == number[None, :]).astype(F32)
    onehot = marks(jnp.concatenate([table[t:], other[t:]], axis=0))
    count = jnp.sum(onehot, axis=0) / nw
    doc = jnp.dot(s, onehot, precision=lax.Precision.HIGHEST, preferred_element_type=F32)

    keep = jnp.concatenate([s[:, :t], doc], axis=1)
    got = to_core(jnp.concatenate([s[:, t:], doc], axis=1))
    blocks = []
    for k in range(0, nb // 2 * nq, nq):
        blocks += [keep[k : k + nq], got[k : k + nq]]
    bit = 1
    while bit < nb:
        swap = (b & bit) != 0
        blocks = [jnp.where(swap, blocks[i ^ bit], blocks[i]) for i in range(nb)]
        bit *= 2
    s = jnp.concatenate(blocks, axis=0)
    s, doc = s[:, :t], s[:, t:]
    doc = jnp.concatenate([doc, jnp.broadcast_to(count[None, :], doc.shape)], axis=1)

    swap = lambda x, y_bit, z_bit: lax.ppermute(
        x,
        ("blk", "width"),
        [(i * nw + k, (i ^ y_bit) * nw + (k ^ z_bit)) for i in range(nb) for k in range(nw)],
    )
    blocks = {i: s[:, i * own : (i + 1) * own] for i in range(nw)}
    y_bits = [1 << i for i in range(1, nb.bit_length() - 1)]
    z_bits = [1 << i for i in range(nw.bit_length() - 1)]
    for y_bit in y_bits[:-1]:
        doc = doc + swap(doc, y_bit, 0)
    for z_bit in z_bits:
        low = (w & z_bit) == 0
        at = [i for i in blocks if not i & z_bit]
        give = [jnp.where(low, blocks[i | z_bit], blocks[i]) for i in at]
        keep = [jnp.where(low, blocks[i], blocks[i | z_bit]) for i in at]
        if z_bit == z_bits[0]:
            cross, up = swap(doc, y_bits[-1], z_bit), swap(doc, y_bits[-1], 0)
        got = swap(jnp.concatenate(give + [doc], axis=1), 0, z_bit)
        blocks = {i: x + got[:, n * own : (n + 1) * own] for n, (i, x) in enumerate(zip(at, keep))}
        side = got[:, len(at) * own :]
        if z_bit == z_bits[0]:
            doc, side = doc + up, side + cross
        doc = doc + side
    scores, doc_scores = finish(blocks[0], doc, docs)
    return (scores.T, doc_scores.T)


def solution(mesh):
    return jax.shard_map(
        per_device,
        mesh=mesh,
        in_specs=(
            P(("groups", "blk"), "width"),
            P(("groups", "blk"), "width", None),
            P(("groups", "blk", "width"), None),
            P(("groups", "blk", "width")),
        ),
        out_specs=(P(("groups", "blk", "width"), None), P("groups", None)),
        check_vma=False,
    )
```

```python
import functools

import jax
import jax.numpy as jnp
from jax import lax
from jax.experimental import pallas as pl
from jax.experimental.pallas import tpu as pltpu
from jax.sharding import PartitionSpec as P

DOC_BLK = 4
LANES = 128
F32, BF16 = jnp.float32, jnp.bfloat16
TILE = 256
PARTS = (2, 4, 8, 16, 16)
VMEM = pl.BlockSpec(memory_space=pltpu.VMEM)
HBM = pl.BlockSpec(memory_space=pltpu.HBM)
PARAMS = pltpu.CompilerParams(vmem_limit_bytes=16 << 20)
COST = pl.CostEstimate(flops=1, bytes_accessed=1, transcendentals=0)


def split(x):
    high = x.astype(BF16)
    return high, (x - high.astype(F32)).astype(BF16)


def in_hbm(x):
    return pltpu.with_memory_space_constraint(x, pltpu.HBM)


def cut_kernel(pieces, g_ref, *refs):
    outs, sems = refs[:-1], refs[-1]
    copies = [
        pltpu.make_async_copy(g_ref.at[:, at : at + n], out, sems.at[i])
        for i, ((at, n), out) in enumerate(zip(pieces, outs))
    ]
    for copy in copies:
        copy.start()
    for copy in copies:
        copy.wait()


def cut(g, pieces):
    nq, _, r = g.shape
    return pl.pallas_call(
        functools.partial(cut_kernel, pieces),
        in_specs=[HBM],
        out_specs=[VMEM] * len(pieces),
        out_shape=[jax.ShapeDtypeStruct((nq, n, r), F32) for _, n in pieces],
        scratch_shapes=[pltpu.SemaphoreType.DMA((len(pieces),))],
        compiler_params=PARAMS,
        cost_estimate=COST,
    )(in_hbm(g))


def weigh(g_ref, step):
    nq, n, _ = g_ref.shape
    return [
        split(jnp.concatenate([g_ref[q, k : k + step] for q in range(nq)], axis=1))
        for k in range(0, n, step)
    ]


def project(a, weights, step):
    dot = functools.partial(jnp.dot, preferred_element_type=F32)
    p = None
    for i, (gh, gl) in enumerate(weights):
        gh, gl = gh[...], gl[...]
        ah, al = split(a[:, i * step : (i + 1) * step])
        if step < 256:
            part = dot(jnp.concatenate([ah, al, ah], axis=1), jnp.concatenate([gh, gh, gl], axis=0))
        else:
            part = dot(ah, gh) + dot(al, gh) + dot(ah, gl)
        p = part if p is None else p + part
    return p


def contract(p, o):
    r = o.shape[1]
    return [jnp.sum(p[:, q : q + r] * o, axis=1) for q in range(0, p.shape[1], r)]


def score_tile(a, weights, o, step):
    return contract(project(a, weights, step), o)


def prepare(g_ref, lead_ref, refs):
    high_ref, low_ref, lead_high_ref, lead_low_ref = refs
    step = high_ref.shape[1]

    @pl.when(pl.program_id(0) == 0)
    def _():
        for k, (gh, gl) in enumerate(weigh(g_ref, step)):
            high_ref[k] = gh
            low_ref[k] = gl
        lead_high_ref[...], lead_low_ref[...] = weigh(lead_ref, lead_ref.shape[1])[0]

    weights = [(high_ref.at[k], low_ref.at[k]) for k in range(high_ref.shape[0])]
    return weights, [(lead_high_ref, lead_low_ref)]


def project_both(a, weights, lead_weights, at):
    step, n = weights[0][0].shape[0], lead_weights[0][0].shape[0]
    return project(a, weights, step), project(a[:, at : at + n], lead_weights, n)


def own_kernel(at, cols, a_ref, g_ref, lead_ref, p_ref, lead_p_ref, stage_ref, *refs):
    weights, lead_weights = prepare(g_ref, lead_ref, refs)
    a = a_ref[...]
    here = pl.ds(pl.multiple_of(pl.program_id(0) * a.shape[0], a.shape[0]), a.shape[0])
    p_ref[here, :], lead_p_ref[here, :] = project_both(a, weights, lead_weights, at)
    stage_ref[here, :] = a[:, cols[0] : cols[1]]


def other_kernel(
    at, cols, a_ref, o_ref, oo_ref, p_ref, lead_p_ref, g_ref, lead_ref, s_ref, stage_ref, *refs
):
    weights, lead_weights = prepare(g_ref, lead_ref, refs)
    a = a_ref[...]
    tile = a.shape[0]
    t = s_ref.shape[1] // 2
    nq = g_ref.shape[0]
    start = pl.program_id(0) * tile

    @pl.when(pl.program_id(0) == 0)
    def _():
        s_ref[...] = jnp.zeros_like(s_ref)

    here = pl.ds(pl.multiple_of(start, tile), tile)
    there = pl.ds(pl.multiple_of(t + start, tile), tile)
    own = p_ref[here, :], lead_p_ref[here, :]
    other = project_both(a, weights, lead_weights, at)
    for to, parts, o in ((here, own, o_ref[here, :]), (there, other, oo_ref[here, :])):
        for i, p in enumerate(parts):
            for q, row in enumerate(contract(p, o)):
                s_ref[i * nq + q, to] = row
    stage_ref[here, :] = a[:, cols[0] : cols[1]]


def near_call(kernel, a, others, g, lead, out):
    t = a.shape[0]
    nq, n, r = g.shape
    tile, step = min(t, TILE), min(n, 512)
    return pl.pallas_call(
        kernel,
        grid=(t // tile,),
        in_specs=[pl.BlockSpec((tile, n), lambda i: (i, 0))] + [VMEM] * (len(others) + 2),
        out_specs=[VMEM] * len(out),
        out_shape=[jax.ShapeDtypeStruct(shape, F32) for shape in out],
        scratch_shapes=[pltpu.VMEM((n // step, step, nq * r), BF16)] * 2
        + [pltpu.VMEM((lead.shape[1], nq * r), BF16)] * 2,
        compiler_params=PARAMS,
        cost_estimate=COST,
    )(in_hbm(a), *others, g, lead)


def stream_kernel(first, *refs):
    a_refs, o_refs, refs = refs[:2], refs[2:4], refs[4:]
    g_ref, prev_ref, s_ref, high_ref, low_ref = refs
    tile, n = a_refs[0].shape
    t = s_ref.shape[1] // 2
    i = pl.program_id(0)
    step = high_ref.shape[1]

    @pl.when(i == 0)
    def _():
        s_ref[...] = prev_ref[...]
        for k, (gh, gl) in enumerate(weigh(g_ref, step)):
            high_ref[k] = gh
            low_ref[k] = gl

    weights = [(high_ref.at[k], low_ref.at[k]) for k in range(n // step)]
    for h in range(2):
        a = a_refs[h][...]
        at = pl.multiple_of(h * t + i * tile, tile)
        o = o_refs[h][pl.ds(pl.multiple_of(i * tile, tile), tile), :]
        for q, row in enumerate(score_tile(a, weights, o, step)):
            s_ref[first + q, pl.ds(at, tile)] += row


def stream_scores(s, activations, outgrads, g, start, first):
    t = activations[0].shape[0]
    nq, n, r = g.shape
    tile = min(t, 512)
    step = min(n, 512)
    col = start // n
    return pl.pallas_call(
        functools.partial(stream_kernel, first),
        grid=(t // tile,),
        in_specs=[pl.BlockSpec((tile, n), lambda i: (i, col))] * 2
        + [VMEM] * 4,
        out_specs=VMEM,
        out_shape=jax.ShapeDtypeStruct(s.shape, F32),
        scratch_shapes=[pltpu.VMEM((n // step, step, nq * r), BF16)] * 2,
        compiler_params=PARAMS,
        cost_estimate=COST,
    )(*[in_hbm(a) for a in activations], *outgrads, g, s)


def staged_kernel(start, first, *refs):
    a_refs, o_refs, (g_ref, prev_ref, s_ref) = refs[:2], refs[2:4], refs[4:]
    n = g_ref.shape[1]
    t = a_refs[0].shape[0]
    tile = min(t, 256)
    weights = weigh(g_ref, n)
    s_ref[...] = prev_ref[...]
    for h in range(2):
        for m in range(0, t, tile):
            a = a_refs[h][m : m + tile, start : start + n]
            at = h * t + m
            for q, row in enumerate(score_tile(a, weights, o_refs[h][m : m + tile, :], n)):
                s_ref[first + q, at : at + tile] += row


def staged_scores(s, stages, outgrads, g, start, first):
    return pl.pallas_call(
        functools.partial(staged_kernel, start, first),
        in_specs=[VMEM] * 6,
        out_specs=VMEM,
        out_shape=jax.ShapeDtypeStruct(s.shape, F32),
        compiler_params=PARAMS,
        cost_estimate=COST,
    )(*stages, *outgrads, g, s)


def finish_kernel(s_ref, doc_ref, scores_ref, doc_scores_ref):
    docs = doc_scores_ref.shape[1]
    scores_ref[...] = s_ref[...]
    doc = doc_ref[...]
    doc_scores_ref[...] = doc[:, :docs] / jnp.sqrt(doc[:, docs : 2 * docs])


def finish(s, doc, docs):
    return pl.pallas_call(
        finish_kernel,
        in_specs=[VMEM] * 2,
        out_specs=[VMEM] * 2,
        out_shape=[
            jax.ShapeDtypeStruct(s.shape, F32),
            jax.ShapeDtypeStruct((s.shape[0], docs), F32),
        ],
        compiler_params=PARAMS,
        cost_estimate=COST,
    )(s, doc)


def per_device(a, g, o, ids):
    nb, nw = lax.axis_size("blk"), lax.axis_size("width")
    b, w = lax.axis_index("blk"), lax.axis_index("width")
    nq, d, r = g.shape
    t = a.shape[0]
    own = o.shape[0]
    docs = DOC_BLK * nb
    pairs = lambda n, k: [(i, i ^ k) for i in range(n)]
    to_core = lambda x: lax.ppermute(x, "blk", pairs(nb, 1))

    def after(x, *others):
        return lax.optimization_barrier((x, *others))[0]

    pieces, at = [], 0
    for part in PARTS:
        n = max(d // part, LANES)
        if at < d:
            pieces.append((at, n))
        at += n
    pieces = pieces[-1:] + pieces[:-1]
    cuts = [g[:, at : at + n] for at, n in pieces[:1]]
    lead = lax.ppermute(cuts[0], "blk", pairs(nb, 2))
    cuts += cut(after(g, cuts[0]), pieces[1:2])
    a_other = to_core(after(a, cuts[0]))
    cuts += cut(after(g, lead), pieces[2:])
    at, last = pieces[0][0], pieces[-1]
    cols = pieces[-2][0], sum(last)
    wide = (t, nq * r), (t, nq * r), (t, cols[1] - cols[0])
    a_own = after(a, lead, *cuts[2:])
    p, lead_p, stage = near_call(functools.partial(own_kernel, at, cols), a_own, [], g, lead, wide)
    sends = [(j, at, x) for j in range(2, nb, 2) for (at, _), x in zip(pieces, cuts)]

    def send(i, *others):
        j, _, x = sends[i]
        return lax.ppermute(after(x, *others), "blk", pairs(nb, j))

    arrived = [lead, lax.ppermute(cuts[1], "blk", pairs(nb, 2)), send(2, lead)]

    rows = own // LANES
    flat = ids.astype(F32).reshape(rows, LANES)
    mine = after(jnp.concatenate([o, flat], axis=0), lead)
    table = after(jnp.zeros((t + t // LANES, LANES), F32), p)
    for k in range(nw):
        got = lax.ppermute(mine, "width", pairs(nw, k)) if k else mine
        src = w ^ k
        table = lax.dynamic_update_slice(table, got[:own], (src * own, 0))
        table = lax.dynamic_update_slice(table, got[own:], (t + src * rows, 0))
    other = to_core(table)

    both, outgrads = [a, a_other], [table, other]
    s, stage_other = near_call(
        functools.partial(other_kernel, at, cols),
        a_other,
        [*outgrads, p, lead_p],
        g,
        lead,
        ((nb // 2 * nq, 2 * t), wide[2]),
    )
    stages = [stage, stage_other]
    arrived.append(send(3, s))
    for i, (j, at, x) in enumerate(sends):
        if i + 4 < len(sends):
            arrived.append(send(i + 4, s))
        first = j // 2 * nq
        if i == 0:
            continue
        if cols[0] <= at < cols[1]:
            s = staged_scores(s, stages, outgrads, arrived[i], at - cols[0], first)
        else:
            s = stream_scores(s, both, outgrads, arrived[i], at, first)

    number = jnp.arange(docs, dtype=F32)
    marks = lambda x: (x.reshape(-1)[:, None] == number[None, :]).astype(F32)
    onehot = marks(jnp.concatenate([table[t:], other[t:]], axis=0))
    count = jnp.sum(onehot, axis=0) / nw
    doc = jnp.dot(s, onehot, precision=lax.Precision.HIGHEST, preferred_element_type=F32)

    keep = jnp.concatenate([s[:, :t], doc], axis=1)
    got = to_core(jnp.concatenate([s[:, t:], doc], axis=1))
    blocks = []
    for k in range(0, nb // 2 * nq, nq):
        blocks += [keep[k : k + nq], got[k : k + nq]]
    bit = 1
    while bit < nb:
        swap = (b & bit) != 0
        blocks = [jnp.where(swap, blocks[i ^ bit], blocks[i]) for i in range(nb)]
        bit *= 2
    s = jnp.concatenate(blocks, axis=0)
    s, doc = s[:, :t], s[:, t:]
    doc = jnp.concatenate([doc, jnp.broadcast_to(count[None, :], doc.shape)], axis=1)

    swap = lambda x, y_bit, z_bit: lax.ppermute(
        x,
        ("blk", "width"),
        [(i * nw + k, (i ^ y_bit) * nw + (k ^ z_bit)) for i in range(nb) for k in range(nw)],
    )
    blocks = {i: s[:, i * own : (i + 1) * own] for i in range(nw)}
    y_bits = [1 << i for i in range(1, nb.bit_length() - 1)]
    z_bits = [1 << i for i in range(nw.bit_length() - 1)]
    for y_bit in y_bits[:-1]:
        doc = doc + swap(doc, y_bit, 0)
    for z_bit in z_bits:
        low = (w & z_bit) == 0
        at = [i for i in blocks if not i & z_bit]
        give = [jnp.where(low, blocks[i | z_bit], blocks[i]) for i in at]
        keep = [jnp.where(low, blocks[i], blocks[i | z_bit]) for i in at]
        if z_bit == z_bits[0]:
            cross, up = swap(doc, y_bits[-1], z_bit), swap(doc, y_bits[-1], 0)
        got = swap(jnp.concatenate(give + [doc], axis=1), 0, z_bit)
        blocks = {i: x + got[:, n * own : (n + 1) * own] for n, (i, x) in enumerate(zip(at, keep))}
        side = got[:, len(at) * own :]
        if z_bit == z_bits[0]:
            doc, side = doc + up, side + cross
        doc = doc + side
    scores, doc_scores = finish(blocks[0], doc, docs)
    return (scores.T, doc_scores.T)


def solution(mesh):
    return jax.shard_map(
        per_device,
        mesh=mesh,
        in_specs=(
            P(("groups", "blk"), "width"),
            P(("groups", "blk"), "width", None),
            P(("groups", "blk", "width"), None),
            P(("groups", "blk", "width")),
        ),
        out_specs=(P(("groups", "blk", "width"), None), P("groups", None)),
        check_vma=False,
    )
```

```python
import functools

import jax
import jax.numpy as jnp
from jax import lax
from jax.experimental import pallas as pl
from jax.experimental.pallas import tpu as pltpu
from jax.sharding import PartitionSpec as P

DOC_BLK = 4
LANES = 128
F32, BF16 = jnp.float32, jnp.bfloat16
TILE = 256
LEADS = 2
PARTS = (2, 4, 16, 16, 16, 16)
VMEM = pl.BlockSpec(memory_space=pltpu.VMEM)
HBM = pl.BlockSpec(memory_space=pltpu.HBM)
PARAMS = pltpu.CompilerParams(vmem_limit_bytes=16 << 20)
COST = pl.CostEstimate(flops=1, bytes_accessed=1, transcendentals=0)


def split(x):
    high = x.astype(BF16)
    return high, (x - high.astype(F32)).astype(BF16)


def in_hbm(x):
    return pltpu.with_memory_space_constraint(x, pltpu.HBM)


def cut_kernel(pieces, g_ref, *refs):
    outs, sems = refs[:-1], refs[-1]
    copies = [
        pltpu.make_async_copy(g_ref.at[:, at : at + n], out, sems.at[i])
        for i, ((at, n), out) in enumerate(zip(pieces, outs))
    ]
    for copy in copies:
        copy.start()
    for copy in copies:
        copy.wait()


def cut(g, pieces):
    nq, _, r = g.shape
    return pl.pallas_call(
        functools.partial(cut_kernel, pieces),
        in_specs=[HBM],
        out_specs=[VMEM] * len(pieces),
        out_shape=[jax.ShapeDtypeStruct((nq, n, r), F32) for _, n in pieces],
        scratch_shapes=[pltpu.SemaphoreType.DMA((len(pieces),))],
        compiler_params=PARAMS,
        cost_estimate=COST,
    )(in_hbm(g))


def weigh(g_ref, step):
    nq, n, _ = g_ref.shape
    return [
        split(jnp.concatenate([g_ref[q, k : k + step] for q in range(nq)], axis=1))
        for k in range(0, n, step)
    ]


def project(a, weights, step):
    dot = functools.partial(jnp.dot, preferred_element_type=F32)
    p = None
    for i, (gh, gl) in enumerate(weights):
        gh, gl = gh[...], gl[...]
        ah, al = split(a[:, i * step : (i + 1) * step])
        if step < 256:
            part = dot(jnp.concatenate([ah, al, ah], axis=1), jnp.concatenate([gh, gh, gl], axis=0))
        else:
            part = dot(ah, gh) + dot(al, gh) + dot(ah, gl)
        p = part if p is None else p + part
    return p


def contract(p, o):
    r = o.shape[1]
    return [jnp.sum(p[:, q : q + r] * o, axis=1) for q in range(0, p.shape[1], r)]


def score_tile(a, weights, o, step):
    return contract(project(a, weights, step), o)


def prepare(g_ref, lead_refs, refs):
    high_ref, low_ref, lead_high_ref, lead_low_ref = refs
    step = high_ref.shape[1]

    @pl.when(pl.program_id(0) == 0)
    def _():
        for k, (gh, gl) in enumerate(weigh(g_ref, step)):
            high_ref[k] = gh
            low_ref[k] = gl
        for k, lead_ref in enumerate(lead_refs):
            lead_high_ref[k], lead_low_ref[k] = weigh(lead_ref, lead_ref.shape[1])[0]

    weights = [(high_ref.at[k], low_ref.at[k]) for k in range(high_ref.shape[0])]
    return weights, [(lead_high_ref.at[k], lead_low_ref.at[k]) for k in range(LEADS)]


def project_both(a, weights, lead_weights, at):
    step, n = weights[0][0].shape[0], lead_weights[0][0].shape[0]
    lead_p = project(a[:, at : at + LEADS * n], lead_weights, n)
    return project(a, weights, step), lead_p


def own_kernel(at, cols, a_ref, g_ref, *refs):
    lead_refs, (p_ref, stage_ref, *refs) = refs[:LEADS], refs[LEADS:]
    weights, lead_weights = prepare(g_ref, lead_refs, refs)
    a = a_ref[...]
    p_ref[...] = jnp.concatenate(project_both(a, weights, lead_weights, at), axis=1)
    stage_ref[...] = a[:, cols[0] : cols[1]]


def other_kernel(at, cols, a_ref, p_ref, o_ref, oo_ref, g_ref, *refs):
    lead_refs, (s_ref, stage_ref, *refs) = refs[:LEADS], refs[LEADS:]
    weights, lead_weights = prepare(g_ref, lead_refs, refs)
    a = a_ref[...]
    tile = a.shape[0]
    t = s_ref.shape[1] // 2
    nq = g_ref.shape[0]
    start = pl.program_id(0) * tile

    @pl.when(pl.program_id(0) == 0)
    def _():
        s_ref[...] = jnp.zeros_like(s_ref)

    here = pl.ds(pl.multiple_of(start, tile), tile)
    there = pl.ds(pl.multiple_of(t + start, tile), tile)
    own = jnp.split(p_ref[...], 2, axis=1)
    other = project_both(a, weights, lead_weights, at)
    for to, parts, o in ((here, own, o_ref[here, :]), (there, other, oo_ref[here, :])):
        for i, p in enumerate(parts):
            for q, row in enumerate(contract(p, o)):
                s_ref[i * nq + q, to] = row
    stage_ref[...] = a[:, cols[0] : cols[1]]


def near_call(kernel, tiled, others, g, leads, whole_out, tiled_out):
    t, n = tiled[0].shape
    nq, _, r = g.shape
    tile, step = min(t, TILE), min(n, 512)
    tiles = lambda width: pl.BlockSpec((tile, width), lambda i: (i, 0))
    return pl.pallas_call(
        kernel,
        grid=(t // tile,),
        in_specs=[tiles(x.shape[1]) for x in tiled] + [VMEM] * (len(others) + 1 + LEADS),
        out_specs=[VMEM] * len(whole_out) + [tiles(width) for width in tiled_out],
        out_shape=[jax.ShapeDtypeStruct(shape, F32) for shape in whole_out]
        + [pltpu.HBM((t, width), F32) for width in tiled_out],
        scratch_shapes=[pltpu.VMEM((n // step, step, nq * r), BF16)] * 2
        + [pltpu.VMEM((LEADS, leads[0].shape[1], nq * r), BF16)] * 2,
        compiler_params=PARAMS,
        cost_estimate=COST,
    )(*[in_hbm(x) for x in tiled], *others, g, *leads)


def stream_kernel(first, *refs):
    a_refs, o_refs, refs = refs[:2], refs[2:4], refs[4:]
    g_ref, prev_ref, s_ref, high_ref, low_ref = refs
    tile, n = a_refs[0].shape
    t = s_ref.shape[1] // 2
    i = pl.program_id(0)
    step = high_ref.shape[1]

    @pl.when(i == 0)
    def _():
        s_ref[...] = prev_ref[...]
        for k, (gh, gl) in enumerate(weigh(g_ref, step)):
            high_ref[k] = gh
            low_ref[k] = gl

    weights = [(high_ref.at[k], low_ref.at[k]) for k in range(n // step)]
    for h in range(2):
        a = a_refs[h][...]
        at = pl.multiple_of(h * t + i * tile, tile)
        o = o_refs[h][pl.ds(pl.multiple_of(i * tile, tile), tile), :]
        for q, row in enumerate(score_tile(a, weights, o, step)):
            s_ref[first + q, pl.ds(at, tile)] += row


def stream_scores(s, activations, outgrads, g, start, first):
    t = activations[0].shape[0]
    nq, n, r = g.shape
    tile = min(t, 512)
    step = min(n, 512)
    col = start // n
    return pl.pallas_call(
        functools.partial(stream_kernel, first),
        grid=(t // tile,),
        in_specs=[pl.BlockSpec((tile, n), lambda i: (i, col))] * 2
        + [VMEM] * 4,
        out_specs=VMEM,
        out_shape=jax.ShapeDtypeStruct(s.shape, F32),
        scratch_shapes=[pltpu.VMEM((n // step, step, nq * r), BF16)] * 2,
        compiler_params=PARAMS,
        cost_estimate=COST,
    )(*[in_hbm(a) for a in activations], *outgrads, g, s)


def staged_kernel(start, first, *refs):
    a_refs, o_refs, (g_ref, prev_ref, s_ref) = refs[:2], refs[2:4], refs[4:]
    n = g_ref.shape[1]
    t = a_refs[0].shape[0]
    tile = min(t, 256)
    weights = weigh(g_ref, n)
    s_ref[...] = prev_ref[...]
    for h in range(2):
        for m in range(0, t, tile):
            a = a_refs[h][m : m + tile, start : start + n]
            at = h * t + m
            for q, row in enumerate(score_tile(a, weights, o_refs[h][m : m + tile, :], n)):
                s_ref[first + q, at : at + tile] += row


def staged_scores(s, stages, outgrads, g, start, first):
    return pl.pallas_call(
        functools.partial(staged_kernel, start, first),
        in_specs=[VMEM] * 6,
        out_specs=VMEM,
        out_shape=jax.ShapeDtypeStruct(s.shape, F32),
        compiler_params=PARAMS,
        cost_estimate=COST,
    )(*stages, *outgrads, g, s)


def finish_kernel(s_ref, doc_ref, scores_ref, doc_scores_ref):
    docs = doc_scores_ref.shape[1]
    scores_ref[...] = s_ref[...]
    doc = doc_ref[...]
    doc_scores_ref[...] = doc[:, :docs] / jnp.sqrt(doc[:, docs : 2 * docs])


def finish(s, doc, docs):
    return pl.pallas_call(
        finish_kernel,
        in_specs=[VMEM] * 2,
        out_specs=[VMEM] * 2,
        out_shape=[
            jax.ShapeDtypeStruct(s.shape, F32),
            jax.ShapeDtypeStruct((s.shape[0], docs), F32),
        ],
        compiler_params=PARAMS,
        cost_estimate=COST,
    )(s, doc)


def per_device(a, g, o, ids):
    nb, nw = lax.axis_size("blk"), lax.axis_size("width")
    b, w = lax.axis_index("blk"), lax.axis_index("width")
    nq, d, r = g.shape
    t = a.shape[0]
    own = o.shape[0]
    docs = DOC_BLK * nb
    pairs = lambda n, k: [(i, i ^ k) for i in range(n)]
    to_core = lambda x: lax.ppermute(x, "blk", pairs(nb, 1))

    def after(x, *others):
        return lax.optimization_barrier((x, *others))[0]

    pieces, at = [], 0
    for part in PARTS:
        n = max(d // part, LANES)
        if at < d:
            pieces.append((at, n))
        at += n
    pieces = pieces[-LEADS:] + pieces[:-LEADS]
    cuts = [g[:, at : at + n] for at, n in pieces[:LEADS]]
    leads = [lax.ppermute(x, "blk", pairs(nb, 2)) for x in cuts]
    lead = leads[0]
    cuts += cut(after(g, cuts[0]), pieces[LEADS : LEADS + 1])
    a_other = to_core(after(a, cuts[0]))
    cuts += cut(after(g, lead), pieces[LEADS + 1 :])
    at = pieces[0][0]
    cols = min(i for i, n in pieces if n <= 512 and i < at), at
    a_own = after(a, lead, *cuts[LEADS + 1 :])
    p, stage = near_call(
        functools.partial(own_kernel, at, cols),
        [a_own],
        [],
        g,
        leads,
        [],
        [2 * nq * r, cols[1] - cols[0]],
    )
    sends = [(j, at, x) for j in range(2, nb, 2) for (at, _), x in zip(pieces, cuts)]

    def send(i, *others):
        j, _, x = sends[i]
        return lax.ppermute(after(x, *others), "blk", pairs(nb, j))

    arrived = leads + [lax.ppermute(cuts[LEADS], "blk", pairs(nb, 2)), send(LEADS + 1, lead)]

    rows = own // LANES
    flat = ids.astype(F32).reshape(rows, LANES)
    mine = after(jnp.concatenate([o, flat], axis=0), lead)
    table = after(jnp.zeros((t + t // LANES, LANES), F32), p)
    for k in range(nw):
        got = lax.ppermute(mine, "width", pairs(nw, k)) if k else mine
        src = w ^ k
        table = lax.dynamic_update_slice(table, got[:own], (src * own, 0))
        table = lax.dynamic_update_slice(table, got[own:], (t + src * rows, 0))
    other = to_core(table)

    both, outgrads = [a, a_other], [table, other]
    s, stage_other = near_call(
        functools.partial(other_kernel, at, cols),
        [a_other, p],
        outgrads,
        g,
        leads,
        [(nb // 2 * nq, 2 * t)],
        [cols[1] - cols[0]],
    )
    stages = [stage, stage_other]
    arrived.append(send(LEADS + 2, s))
    for i, (j, at, x) in enumerate(sends):
        if i + LEADS + 3 < len(sends):
            arrived.append(send(i + LEADS + 3, s))
        first = j // 2 * nq
        if i < LEADS:
            continue
        if cols[0] <= at < cols[1]:
            s = staged_scores(s, stages, outgrads, arrived[i], at - cols[0], first)
        else:
            s = stream_scores(s, both, outgrads, arrived[i], at, first)

    number = jnp.arange(docs, dtype=F32)
    marks = lambda x: (x.reshape(-1)[:, None] == number[None, :]).astype(F32)
    onehot = marks(jnp.concatenate([table[t:], other[t:]], axis=0))
    count = jnp.sum(onehot, axis=0) / nw
    doc = jnp.dot(s, onehot, precision=lax.Precision.HIGHEST, preferred_element_type=F32)

    keep = jnp.concatenate([s[:, :t], doc], axis=1)
    got = to_core(jnp.concatenate([s[:, t:], doc], axis=1))
    blocks = []
    for k in range(0, nb // 2 * nq, nq):
        blocks += [keep[k : k + nq], got[k : k + nq]]
    bit = 1
    while bit < nb:
        swap = (b & bit) != 0
        blocks = [jnp.where(swap, blocks[i ^ bit], blocks[i]) for i in range(nb)]
        bit *= 2
    s = jnp.concatenate(blocks, axis=0)
    s, doc = s[:, :t], s[:, t:]
    doc = jnp.concatenate([doc, jnp.broadcast_to(count[None, :], doc.shape)], axis=1)

    swap = lambda x, y_bit, z_bit: lax.ppermute(
        x,
        ("blk", "width"),
        [(i * nw + k, (i ^ y_bit) * nw + (k ^ z_bit)) for i in range(nb) for k in range(nw)],
    )
    blocks = {i: s[:, i * own : (i + 1) * own] for i in range(nw)}
    y_bits = [1 << i for i in range(1, nb.bit_length() - 1)]
    z_bits = [1 << i for i in range(nw.bit_length() - 1)]
    for y_bit in y_bits[:-1]:
        doc = doc + swap(doc, y_bit, 0)
    for z_bit in z_bits:
        low = (w & z_bit) == 0
        at = [i for i in blocks if not i & z_bit]
        give = [jnp.where(low, blocks[i | z_bit], blocks[i]) for i in at]
        keep = [jnp.where(low, blocks[i], blocks[i | z_bit]) for i in at]
        if z_bit == z_bits[0]:
            cross, up = swap(doc, y_bits[-1], z_bit), swap(doc, y_bits[-1], 0)
        got = swap(jnp.concatenate(give + [doc], axis=1), 0, z_bit)
        blocks = {i: x + got[:, n * own : (n + 1) * own] for n, (i, x) in enumerate(zip(at, keep))}
        side = got[:, len(at) * own :]
        if z_bit == z_bits[0]:
            doc, side = doc + up, side + cross
        doc = doc + side
    scores, doc_scores = finish(blocks[0], doc, docs)
    return (scores.T, doc_scores.T)


def solution(mesh):
    return jax.shard_map(
        per_device,
        mesh=mesh,
        in_specs=(
            P(("groups", "blk"), "width"),
            P(("groups", "blk"), "width", None),
            P(("groups", "blk", "width"), None),
            P(("groups", "blk", "width")),
        ),
        out_specs=(P(("groups", "blk", "width"), None), P("groups", None)),
        check_vma=False,
    )
```
